128 devices in a mesh: grp: 4 (over x), tile: 32 (over z, y, core).
Axes of the slice: x: 4, y: 4, z: 4, core: 2. Of those that a mesh axis runs over, the one named last changes fastest.
Arguments:
- atmos: float32 [16, 64, 8192], P(None, 'grp', 'tile'), may hold values from -6 to 6
- diffusivity: float32 [64, 8192], P('grp', 'tile'), may hold values from 0.02 to 0.2
- sea_atm: int32 [64, 8192], P('grp', 'tile'), may hold values 0 or 1
- flux_weight: float32 [12, 16], replicated, may hold values from -1.5 to 1.5
- block_owner: int32 [16384, 1], P(('grp', 'tile')), may hold values from 0 to 127; in each aligned block of 128 rows (0 to 127, 128 to 255, ...) at most 2 rows name the same one
- entry_count: int32 [16384], P(('grp', 'tile')), may hold values from 64 to 128, as said below
- source_col: int32 [16384, 128], P(('grp', 'tile')), may hold values from 0 to 4095
- dest_col: int32 [16384, 128], P(('grp', 'tile')), may hold values from 0 to 1023
- margin: float32 [16384, 128], P(('grp', 'tile')), may hold values from 0.1 to 0.6
- ocean: float32 [8, 131072], P(None, ('grp', 'tile')), may hold values from -6 to 6
- sea_ocean: int32 [131072], P(('grp', 'tile')), may hold values 0 or 1
- couple: float32 [8, 12], replicated, may hold values from -1.75 to 1.75
- surface_weight: float32 [6, 8], replicated, may hold values from -2 to 2
Outputs:
- atmos_out: float32 [16, 64, 8192], P(None, 'grp', 'tile')
- ocean_out: float32 [8, 131072], P(None, ('grp', 'tile'))
- atm_surface: float32 [6, 64, 8192], P(None, 'grp', 'tile')
The draws below stay inside these ranges and needn't reach their ends.
Inputs may be any that keep to these rules, and one draw needn't show every extreme that they name: `block_owner`: among the blocks of one device, at most 2 have the same owner. `entry_count`: the first block of every device is full.
All inputs are finite; a program needn't handle non-finite values. No bound on the sum of `sea_atm` or of `sea_ocean` on one device may be relied on, other than what follows from the above.
Results may differ from the reference program's by a relative error of at most 0.0033.
Values may be sent and summed in bfloat16 or wider, within the bound.
A program may use at most 64 MiB of HBM per device.

```python
import math
import jax
import jax.numpy as jnp
import numpy as np
from jax import lax

CH = 16
FLUXES = 12
SURF = 6
OCH = 8
STEPS = 2
ENTRIES = 128
NY_D = 16
NX_D = 256
BLK_DEV = 128
COLS = 4096
OC_DEV = 1024
CAP = 2
BLOCKS = 16384
NY = 64
NX = 8192
OC = 131072
N_GRP = 4
N_TILE = 32
DEVICES = 128


def draw_entry_count(key, part):
    counts = jax.random.randint(jax.random.fold_in(key, 17), (BLOCKS,), ENTRIES // 2, ENTRIES + 1)
    return counts.at[::BLK_DEV].set(ENTRIES).astype(jnp.int32)


def with_ends(drawn, stream_key, smallest, top_value):
    extent = drawn.shape
    index_at = [jax.random.randint(jax.random.fold_in(stream_key, axis), (), 0, extent[axis]) for axis in range(len(extent))]
    drawn = drawn.at[tuple(index_at)].set(smallest)
    longest = extent.index(max(extent))
    index_at[longest] = (index_at[longest] + 1) % extent[longest]
    return drawn.at[tuple(index_at)].set(top_value)


def shard_levels(own_key, shape, cuts, low, high):
    gain, own = 1.0, jax.random.fold_in(own_key, 6)
    for axis_at, blocks in cuts:
        heights = jnp.exp(jax.random.uniform(jax.random.fold_in(own, axis_at), (blocks,), jnp.float32, low / len(cuts), high / len(cuts)))
        gain = gain * jnp.repeat(heights, shape[axis_at] // blocks).reshape([-1 if axis == axis_at else 1 for axis in range(len(shape))])
    return gain


def shared_out(stream_key, own, number, rows, amount, top, bound, slope):
    ranking = jax.random.permutation(stream_key, amount)
    heavy_load, usual = portions_of(amount, rows * top, bound, slope, True), portions_of(amount, rows * top, bound, slope, False)
    places = jnp.arange(amount)

    def named(tallies, offset_by):
        used = int((tallies > 0).sum())
        fixed = max(1, used // 4)
        moved = fixed + (places - fixed + offset_by * (used - fixed)) % max(1, amount - fixed)
        return jnp.zeros((amount,), jnp.int32).at[ranking[jnp.where(places < fixed, places, moved)]].set(jnp.asarray(tallies, jnp.int32))

    tallies = jnp.where(number % 4 == 0, named(heavy_load, number // 4), named(usual, number - number // 4 - 1))
    mixed = jax.random.permutation(jax.random.fold_in(own, 3), amount)
    donor, sink = mixed[0:amount // 2 * 2:2], mixed[1:amount // 2 * 2:2]
    room = jnp.minimum(tallies[donor] - 1, bound - tallies[sink]) // 2
    room = jnp.where((donor == ranking[0]) | (sink == ranking[0]) | (tallies[sink] == 0), 0, jnp.maximum(room, 0))
    moved = jax.random.randint(jax.random.fold_in(own, 4), (amount // 2,), 0, 1 << 20) % (room + 1)
    tallies = tallies.at[donor].add(-moved).at[sink].add(moved)
    labels = jnp.searchsorted(jnp.cumsum(tallies), jnp.arange(rows * top), side="right").astype(jnp.int32)
    grid = labels.reshape(top, rows).T
    grid = grid[jax.random.permutation(jax.random.fold_in(own, 1), rows)]
    offset_by = jax.random.randint(jax.random.fold_in(own, 2), (rows, 1), 0, top)
    return jnp.take_along_axis(grid, (jnp.arange(top)[None, :] + offset_by) % top, axis=1)


def portions_of(number_of, total, limit, skew, full):
    weights = [(1 << 20) // math.isqrt(grade ** skew) + 1 for grade in range(1, number_of + 1)]
    largest = limit if full else min(limit, max(-(-total // number_of), total * weights[0] // sum(weights)))
    least = 1 if total - largest >= number_of - 1 else 0
    holding, surplus = [largest] + [least] * (number_of - 1), total - largest - least * (number_of - 1)
    while surplus > 0:
        candidates = [i for i in range(1, number_of) if holding[i] < largest] or [i for i in range(1, number_of) if holding[i] < limit]
        pool, left = sum([weights[i] for i in candidates]), surplus
        for i in candidates:
            extra = min(limit - holding[i], max(1, left * weights[i] // pool), surplus)
            holding[i] = holding[i] + extra
            surplus = surplus - extra
    return np.array(holding)


def bell_draw(stream_key, dims, spread, reach, cuts=(), held_as=jnp.bfloat16):
    gain = shard_levels(stream_key, dims, cuts, -0.22, 0.18) if cuts else 1.0
    result = jax.random.normal(stream_key, dims, jnp.float32) * spread * gain
    return jnp.minimum(jnp.maximum(result, -reach), reach).astype(held_as)


def setup_inputs(seed: int = 0) -> dict:
    splits = jax.random.split(jax.random.key(seed), 14)
    atmos = bell_draw(splits[0], (CH, NY, NX), 1.0, 6.0, ((1, 4), (2, 32)), jnp.float32)
    diffusivity = jnp.clip(jnp.exp(math.log(0.2) - 2.3025851 * jax.random.uniform(splits[1], (NY, NX), jnp.float32) ** shard_levels(splits[1], (NY, NX), ((0, 4), (1, 32)), -0.2, 0.2)), 0.02, 0.2)
    sea_atm = with_ends((jax.random.randint(splits[2], (NY, NX), 0, 4) < 3).astype(jnp.int32), jax.random.fold_in(splits[2], 1), 0, 1)
    flux_weight = bell_draw(splits[3], (FLUXES, CH), CH ** -0.5, 1.5, (), jnp.float32)
    block_owner_keys = jax.random.split(jax.random.fold_in(splits[4], 1), BLOCKS // BLK_DEV)
    block_owner_turns = jax.random.permutation(jax.random.fold_in(splits[4], 3), BLOCKS // BLK_DEV)
    block_owner = jax.vmap(lambda own, number: shared_out(jax.random.fold_in(splits[4], 2), own, number, BLK_DEV, DEVICES, 1, CAP, 2))(block_owner_keys, block_owner_turns).reshape((BLOCKS, 1))
    entry_count = draw_entry_count(jax.random.fold_in(splits[13], 71), 0)
    source_col = with_ends(jax.random.randint(splits[6], (BLOCKS, ENTRIES), 0, COLS), jax.random.fold_in(splits[6], 1), 0, COLS - 1).astype(jnp.int32)
    dest_col = with_ends(jax.random.randint(splits[7], (BLOCKS, ENTRIES), 0, OC_DEV), jax.random.fold_in(splits[7], 1), 0, OC_DEV - 1).astype(jnp.int32)
    margin = jnp.clip(0.1 + 0.5 * jax.random.uniform(splits[8], (BLOCKS, ENTRIES), jnp.float32) ** shard_levels(splits[8], (BLOCKS, ENTRIES), ((0, 128),), -0.2, 0.2), 0.1, 0.6)
    ocean = bell_draw(splits[9], (OCH, OC), 1.0, 6.0, ((1, 128),), jnp.float32)
    sea_ocean = with_ends((jax.random.randint(splits[10], (OC,), 0, 4) < 3).astype(jnp.int32), jax.random.fold_in(splits[10], 1), 0, 1)
    couple = bell_draw(splits[11], (OCH, FLUXES), FLUXES ** -0.5, 1.75, (), jnp.float32)
    surface_weight = bell_draw(splits[12], (SURF, OCH), OCH ** -0.5, 2.0, (), jnp.float32)
    return {"atmos": atmos, "diffusivity": diffusivity, "sea_atm": sea_atm, "flux_weight": flux_weight, "block_owner": block_owner, "entry_count": entry_count, "source_col": source_col, "dest_col": dest_col, "margin": margin, "ocean": ocean, "sea_ocean": sea_ocean, "couple": couple, "surface_weight": surface_weight}


def stencil_step(state, diffusivity):
    padded = jnp.pad(state, ((0, 0), (1, 1), (1, 1)))
    center = padded[:, 1:-1, 1:-1]
    laplace = padded[:, 2:, 1:-1] + padded[:, :-2, 1:-1] + padded[:, 1:-1, 2:] + padded[:, 1:-1, :-2] - 4.0 * center
    return center + diffusivity[None] * laplace


def to_devices(field):
    chans = field.shape[0]
    split = field.reshape(chans, N_GRP, NY_D, N_TILE, NX_D)
    return jnp.transpose(split, (1, 3, 0, 2, 4)).reshape(N_GRP * N_TILE, chans, NY_D * NX_D)


def from_devices(stacked):
    chans = stacked.shape[1]
    split = stacked.reshape(N_GRP, N_TILE, chans, NY_D, NX_D)
    return jnp.transpose(split, (2, 0, 3, 1, 4)).reshape(chans, N_GRP * NY_D, N_TILE * NX_D)


def reference(atmos, diffusivity, sea_atm, flux_weight, block_owner, entry_count, source_col, dest_col, margin, ocean, sea_ocean, couple, surface_weight):
    hi = lax.Precision.HIGHEST
    state = atmos
    for step in range(STEPS):
        state = stencil_step(state, diffusivity)
    mixed = jnp.einsum("fc,cyx->fyx", flux_weight, state, precision=hi)
    fluxes = jnp.where(sea_atm[None] > 0, jnp.tanh(mixed), jnp.float32(0.0))
    flux_dev = to_devices(fluxes)
    devices = N_GRP * N_TILE
    live = lax.iota(jnp.int32, ENTRIES)[None, :] < entry_count[:, None]
    w_live = jnp.where(live, margin, jnp.float32(0.0)).reshape(devices, BLK_DEV, ENTRIES)
    owners = block_owner[:, 0].reshape(devices, BLK_DEV)
    sources = source_col.reshape(devices, BLK_DEV, ENTRIES)
    global_dest = (owners[:, :, None] * OC_DEV + dest_col.reshape(devices, BLK_DEV, ENTRIES)).astype(jnp.int32)

    def send_one(carry, items):
        flux_here, src_here, dst_here, w_here = items
        contrib = (flux_here[:, src_here] * w_here[None]).astype(jnp.bfloat16)
        carry = carry.at[:, dst_here.reshape(-1)].add(contrib.reshape(FLUXES, -1).astype(jnp.float32))
        return carry, None

    start = jnp.zeros((FLUXES, OC_DEV * devices), jnp.float32)
    ocean_flux, unused = lax.scan(send_one, start, (flux_dev, sources, global_dest, w_live))
    ocean_out = ocean + jnp.where(sea_ocean[None] > 0, jnp.dot(couple, ocean_flux, precision=hi), jnp.float32(0.0))
    surface = jnp.tanh(jnp.dot(surface_weight, ocean_out, precision=hi)).astype(jnp.bfloat16)

    def back_one(carry, items):
        src_here, dst_here, w_here = items
        values = surface[:, dst_here].astype(jnp.float32) * w_here[None]
        summed = jnp.zeros((SURF, NY_D * NX_D), jnp.float32).at[:, src_here.reshape(-1)].add(values.reshape(SURF, -1))
        return carry, summed

    unused2, per_device = lax.scan(back_one, jnp.float32(0.0), (sources, global_dest, w_live))
    atm_surface = jnp.where(sea_atm[None] > 0, from_devices(per_device), jnp.float32(0.0))
    return state, ocean_out, atm_surface
```

```python
import functools

import jax
import jax.numpy as jnp
from jax import lax
from jax.experimental import pallas as pl
from jax.experimental.pallas import tpu as pltpu
from jax.sharding import PartitionSpec as P

MESH = pl.DeviceIdType.MESH
F32, BF16, I32 = jnp.float32, jnp.bfloat16, jnp.int32
NT = (((1,), (1,)), ((), ()))
G = 8


def iota(shape, dim):
    return lax.broadcasted_iota(I32, shape, dim)


def rows_of(row, count):
    return jnp.broadcast_to(row, (count, row.shape[1]))


def remote(src, dst, send_sem, recv_sem, device):
    return pltpu.make_async_remote_copy(
        src_ref=src,
        dst_ref=dst,
        send_sem=send_sem,
        recv_sem=recv_sem,
        device_id=device,
        device_id_type=MESH,
    )


def kernel(
    grps,
    tiles,
    atmos,
    kappa,
    sea_atm,
    flux_w,
    owner,
    count,
    source,
    dest,
    margin,
    ocean,
    sea_oc,
    couple,
    surf_w,
    atmos_out,
    ocean_out,
    atm_surf,
    mid,
    row_send,
    row_recv,
    col_send,
    col_recv,
    src_hi,
    src_lo,
    dst_hi,
    dst_lo,
    weight,
    hot_src,
    hot_dst,
    table32,
    table,
    fwd_send,
    fwd_recv,
    spread,
    surf32,
    back_send,
    back_recv,
    spread2,
    total,
    summed,
    halo_ss,
    halo_rs,
    fwd_ss,
    fwd_rs,
    back_ss,
    back_rs,
):
    devices = grps * tiles
    groups = devices // G
    width = G * 256
    g, t = lax.axis_index("grp"), lax.axis_index("tile")
    me = g * tiles + t

    def at(place):
        place = lax.rem(place, devices)
        return (place // tiles, lax.rem(place, tiles))

    barrier = pltpu.get_barrier_semaphore()

    @pl.loop(1, devices)
    def _(k):
        pl.semaphore_signal(barrier, inc=1, device_id=at(me + k), device_id_type=MESH)

    blocks = owner.shape[1]
    own_row = owner[...]
    own_here = jnp.broadcast_to(own_row, (blocks, blocks)).astype(F32)
    own_col = jnp.transpose(own_here)
    cnt_col = jnp.transpose(jnp.broadcast_to(count[...], (blocks, blocks)).astype(F32))
    before = iota((blocks, blocks), 0) < iota((blocks, blocks), 1)
    same = jnp.where((own_here == own_col) & before, F32(1), F32(0))
    rank = jnp.sum(same, axis=0, keepdims=True).astype(I32)
    ahead = own_row - me
    ahead = jnp.where(ahead < 0, ahead + devices, ahead)
    slot = ahead * 2 + rank
    place = jnp.where(
        iota((2 * devices, blocks), 0) == jnp.broadcast_to(slot, (2 * devices, blocks)), F32(1), F32(0)
    ).astype(BF16)

    def placed(values):
        return jnp.dot(place, values.astype(BF16), preferred_element_type=F32)

    src = source[...]
    src_hi[...] = placed((src >> 8).astype(F32))
    src_lo[...] = placed((src & 255).astype(F32))
    dst = dest[...]
    dst_hi[...] = placed((dst >> 7).astype(F32))
    dst_lo[...] = placed((dst & 127).astype(F32))
    lanes = iota((blocks, 128), 1).astype(F32)
    live = jnp.where(lanes < cnt_col[:, :1], margin[...], F32(0))
    first = live.astype(BF16).astype(F32)
    rest = live - first
    second = rest.astype(BF16).astype(F32)
    third = rest - second
    weight[...] = placed(first) + placed(second) + placed(third)

    ids16 = (iota((16, 16, 128), 0) * 16 + iota((16, 16, 128), 1)).astype(F32).astype(BF16)
    ids8 = (iota((8, 16, 128), 0) * 16 + iota((8, 16, 128), 1)).astype(F32).astype(BF16)
    one, zero = jnp.ones((16, 128), BF16), jnp.zeros((16, 128), BF16)

    @pl.loop(0, devices // 4)
    def _(i):
        low = src_lo[pl.ds(pl.multiple_of(i * 8, 8), 8), :]
        for j in range(8):
            lo = rows_of(low[j : j + 1], 16).astype(BF16)
            hot = jnp.where(ids16 == lo[None], one[None], zero[None])
            hot_src[:, pl.ds(pl.multiple_of(i * 1024 + j * 128, 128), 128)] = hot.reshape(256, 128)

    pl.semaphore_wait(barrier, devices - 1)

    rows, cols = atmos.shape[1], atmos.shape[2]
    chans = atmos.shape[0]
    row_id, col_id = iota((rows, cols), 0), iota((rows, cols), 1)
    lane = iota((rows, 128), 1)
    beside = (
        (lax.rem(g + grps - 1, grps), t),
        (lax.rem(g + 1, grps), t),
        (g, lax.rem(t + tiles - 1, tiles)),
        (g, lax.rem(t + 1, tiles)),
    )
    edge = (g == 0, g == grps - 1, t == 0, t == tiles - 1)
    diffusion = kappa[...]
    for step in range(2):
        state = atmos if step == 0 else mid
        west = jnp.zeros((rows, 128), F32)
        east = jnp.zeros((rows, 128), F32)
        for ch in range(chans):
            x = state[ch]
            row_send[step, 0, ch : ch + 1, :] = x[0:1]
            row_send[step, 1, ch : ch + 1, :] = x[rows - 1 : rows]
            west = jnp.where(lane == ch, x[:, 0:1], west)
            east = jnp.where(lane == ch, x[:, cols - 1 : cols], east)
        col_send[step, 0] = west
        col_send[step, 1] = east
        copies = []
        for side in range(4):
            sent, got = (row_send, row_recv) if side < 2 else (col_send, col_recv)
            copies.append(
                remote(
                    sent.at[step, side % 2],
                    got.at[step, 1 - side % 2],
                    halo_ss.at[step, side],
                    halo_rs.at[step, side],
                    beside[side],
                )
            )
        for copy in copies:
            copy.start()
        for copy in copies:
            copy.wait()
        north = jnp.where(edge[0], F32(0), row_recv[step, 0])
        south = jnp.where(edge[1], F32(0), row_recv[step, 1])
        west = jnp.where(edge[2], F32(0), col_recv[step, 0])
        east = jnp.where(edge[3], F32(0), col_recv[step, 1])
        for ch in range(chans):
            x = state[ch]
            up = jnp.where(row_id == 0, north[ch : ch + 1], pltpu.roll(x, 1, 0))
            down = jnp.where(row_id == rows - 1, south[ch : ch + 1], pltpu.roll(x, rows - 1, 0))
            left = jnp.where(col_id == 0, west[:, ch : ch + 1], pltpu.roll(x, 1, 1))
            right = jnp.where(col_id == cols - 1, east[:, ch : ch + 1], pltpu.roll(x, cols - 1, 1))
            new = x + diffusion * (down + up + right + left - 4.0 * x)
            if step == 0:
                mid[ch] = new
            else:
                atmos_out[ch] = new

    sea = sea_atm[...] > 0
    for f in range(12):
        mixed = flux_w[f, 0] * atmos_out[0]
        for ch in range(1, chans):
            mixed = mixed + flux_w[f, ch] * atmos_out[ch]
        flux = jnp.where(sea, jnp.tanh(mixed), F32(0))
        for half in range(2):
            part = flux[:, half * 128 : half * 128 + 128]
            if f < 8:
                table32[half, pl.ds(f, 16, stride=8), :] = part
            else:
                table32[half, pl.ds(128 + f - 8, 16, stride=4), :] = part
    for half in range(2):
        full = table32[half]
        top = full.astype(BF16)
        table[:, half * 128 : half * 128 + 128] = top
        table[:, 256 + half * 128 : 384 + half * 128] = (full - top.astype(F32)).astype(BF16)

    sub = iota((8, 128), 0)
    odd = jnp.where(sub >= 4, F32(1), F32(0))

    @pl.loop(0, groups)
    def _(i):
        hot = hot_src[:, pl.ds(pl.multiple_of(i * width, width), width)]
        found = jnp.dot(table[...], jnp.concatenate([hot, hot], axis=0), preferred_element_type=F32)
        here = pl.ds(pl.multiple_of(i * 2 * G, 2 * G), 2 * G)
        hi, w, dh, dl = src_hi[here, :], weight[here, :], dst_hi[here, :], dst_lo[here, :]
        for j in range(2 * G):
            mine = found[:, j * 128 : j * 128 + 128]
            h = rows_of(hi[j : j + 1], 8)
            wide = mine[0:8]
            for v in range(1, 16):
                wide = jnp.where(h == v, mine[v * 8 : v * 8 + 8], wide)
            h = h - odd
            thin = jnp.zeros((8, 128), F32)
            for v in range(8):
                thin = jnp.where(h == 2 * v, mine[128 + v * 8 : 136 + v * 8], thin)
            thin = thin + pltpu.roll(thin, 4, 0)
            scale = rows_of(w[j : j + 1], 8)
            thin = jnp.where(sub == 4, rows_of(dh[j : j + 1], 8), thin * scale)
            thin = jnp.where(sub == 5, rows_of(dl[j : j + 1], 8), thin)
            fwd_send[i * G + j // 2, j % 2] = jnp.concatenate([wide * scale, thin], axis=0).astype(BF16)
        for j in range(G):
            k = i * G + j

            @pl.when(k > 0)
            def _():
                remote(
                    fwd_send.at[k], fwd_recv.at[k], fwd_ss.at[k], fwd_rs.at[k], at(me + k)
                ).start()

    fwd_recv[0] = fwd_send[0]

    total[...] = jnp.zeros_like(total)

    @pl.loop(0, groups)
    def _(i):
        for j in range(G):
            k = i * G + j

            @pl.when(k > 0)
            def _():
                remote(
                    fwd_send.at[k], fwd_recv.at[k], fwd_ss.at[k], fwd_rs.at[k], at(me + k)
                ).wait_recv()

        for j in range(2 * G):
            tile = fwd_recv[i * G + j // 2, j % 2]
            wide = tile.astype(F32)
            hi = rows_of(wide[12:13], 16).astype(BF16)
            lo = rows_of(wide[13:14], 16).astype(BF16)
            for v in range(8):
                spread[v * 16 : v * 16 + 16, j * 128 : j * 128 + 128] = jnp.where(hi == v, tile, zero)
            hot = jnp.where(ids8 == lo[None], one[None], zero[None])
            hot_dst[:, pl.ds(pl.multiple_of(i * width + j * 128, 128), 128)] = hot.reshape(128, 128)
        total[...] += lax.dot_general(
            spread[...],
            hot_dst[:, pl.ds(pl.multiple_of(i * width, width), width)],
            NT,
            preferred_element_type=F32,
        )

    surf32[...] = jnp.zeros_like(surf32)
    for h in range(8):
        here = slice(h * 128, h * 128 + 128)
        flux = total[h * 16 : h * 16 + 16, :]
        added = couple[:, 0:1] * flux[0:1]
        for f in range(1, 12):
            added = added + couple[:, f : f + 1] * flux[f : f + 1]
        new = ocean[:, here] + jnp.where(sea_oc[:, here] > 0, added, F32(0))
        ocean_out[:, here] = new
        field = surf_w[:, 0:1] * new[0:1]
        for o in range(1, 8):
            field = field + surf_w[:, o : o + 1] * new[o : o + 1]
        surf32[h * 8 : h * 8 + 6, :] = jnp.tanh(field)
    surface = surf32[...].astype(BF16)

    @pl.loop(0, groups)
    def _(i):
        found = jnp.dot(
            surface,
            hot_dst[:, pl.ds(pl.multiple_of(i * width, width), width)],
            preferred_element_type=F32,
        )
        for j in range(G):
            k = i * G + j
            both = []
            for part in range(2):
                mine = found[:, (2 * j + part) * 128 : (2 * j + part) * 128 + 128]
                tile = fwd_recv[k, part].astype(F32)
                h = rows_of(tile[12:13], 8)
                got = mine[0:8]
                for v in range(1, 8):
                    got = jnp.where(h == v, mine[v * 8 : v * 8 + 8], got)
                both.append(got)
            back_send[k] = jnp.concatenate(both, axis=0).astype(BF16)
        for j in range(G):
            k = i * G + j

            @pl.when(k > 0)
            def _():
                remote(
                    back_send.at[k], back_recv.at[k], back_ss.at[k], back_rs.at[k], at(me + devices - k)
                ).start()

    back_recv[0] = back_send[0]

    summed[...] = jnp.zeros_like(summed)

    @pl.loop(0, groups)
    def _(i):
        for j in range(G):
            k = i * G + j

            @pl.when(k > 0)
            def _():
                remote(
                    back_send.at[k], back_recv.at[k], back_ss.at[k], back_rs.at[k], at(me + devices - k)
                ).wait_recv()

        here = pl.ds(pl.multiple_of(i * 2 * G, 2 * G), 2 * G)
        hi, w = src_hi[here, :], weight[here, :]
        for j in range(2 * G):
            both = back_recv[i * G + j // 2].astype(F32)
            value = both[(j % 2) * 8 : (j % 2) * 8 + 8] * rows_of(w[j : j + 1], 8)
            top = value.astype(BF16).astype(F32)
            pair = jnp.concatenate([top, value - top], axis=0).astype(BF16)
            h = rows_of(hi[j : j + 1], 16).astype(BF16)
            for v in range(16):
                spread2[v * 16 : v * 16 + 16, j * 128 : j * 128 + 128] = jnp.where(h == v, pair, zero)
        summed[...] += lax.dot_general(
            spread2[...],
            hot_src[:, pl.ds(pl.multiple_of(i * width, width), width)],
            NT,
            preferred_element_type=F32,
        )

    for half in range(2):
        here = slice(half * 128, half * 128 + 128)
        for h in range(16):
            table32[half, h * 8 : h * 8 + 8, :] = (
                summed[h * 16 : h * 16 + 8, here] + summed[h * 16 + 8 : h * 16 + 16, here]
            )
        for s in range(6):
            atm_surf[s, :, here] = jnp.where(
                sea[:, here], table32[half, pl.ds(s, 16, stride=8), :], F32(0)
            )

    @pl.loop(1, devices)
    def _(k):
        remote(fwd_send.at[k], fwd_recv.at[k], fwd_ss.at[k], fwd_rs.at[k], at(me + k)).wait_send()
        remote(
            back_send.at[k], back_recv.at[k], back_ss.at[k], back_rs.at[k], at(me + devices - k)
        ).wait_send()


def on_device(grps, tiles, *args):
    (
        atmos,
        diffusivity,
        sea_atm,
        flux_weight,
        block_owner,
        entry_count,
        source_col,
        dest_col,
        margin,
        ocean,
        sea_ocean,
        couple,
        surface_weight,
    ) = args
    devices = grps * tiles
    slots = 2 * devices
    vmem = pl.BlockSpec(memory_space=pltpu.VMEM)
    smem = pl.BlockSpec(memory_space=pltpu.SMEM)
    chans, rows, cols = atmos.shape
    dma = pltpu.SemaphoreType.DMA
    return pl.pallas_call(
        functools.partial(kernel, grps, tiles),
        out_shape=(
            jax.ShapeDtypeStruct(atmos.shape, F32),
            jax.ShapeDtypeStruct(ocean.shape, F32),
            jax.ShapeDtypeStruct((6, rows, cols), F32),
        ),
        in_specs=[vmem, vmem, vmem, smem] + [vmem] * 9,
        out_specs=(vmem, vmem, vmem),
        scratch_shapes=[
            pltpu.VMEM((chans, rows, cols), F32),
            pltpu.VMEM((2, 2, chans, cols), F32),
            pltpu.VMEM((2, 2, chans, cols), F32),
            pltpu.VMEM((2, 2, rows, 128), F32),
            pltpu.VMEM((2, 2, rows, 128), F32),
            pltpu.VMEM((slots, 128), F32),
            pltpu.VMEM((slots, 128), F32),
            pltpu.VMEM((slots, 128), F32),
            pltpu.VMEM((slots, 128), F32),
            pltpu.VMEM((slots, 128), F32),
            pltpu.VMEM((256, slots * 128), BF16),
            pltpu.VMEM((128, slots * 128), BF16),
            pltpu.VMEM((2, 192, 128), F32),
            pltpu.VMEM((192, 512), BF16),
            pltpu.VMEM((devices, 2, 16, 128), BF16),
            pltpu.VMEM((devices, 2, 16, 128), BF16),
            pltpu.VMEM((128, G * 256), BF16),
            pltpu.VMEM((64, 128), F32),
            pltpu.VMEM((devices, 16, 128), BF16),
            pltpu.VMEM((devices, 16, 128), BF16),
            pltpu.VMEM((256, G * 256), BF16),
            pltpu.VMEM((128, 128), F32),
            pltpu.VMEM((256, 256), F32),
            dma((2, 4)),
            dma((2, 4)),
            dma((devices,)),
            dma((devices,)),
            dma((devices,)),
            dma((devices,)),
        ],
        compiler_params=pltpu.CompilerParams(
            collective_id=0, has_side_effects=True, vmem_limit_bytes=56 * 1024 * 1024
        ),
    )(
        atmos,
        diffusivity,
        sea_atm,
        flux_weight,
        block_owner.reshape(1, -1),
        entry_count.reshape(1, -1),
        source_col,
        dest_col,
        margin,
        ocean,
        sea_ocean.reshape(1, -1),
        couple,
        surface_weight,
    )


def solution(mesh):
    placed = (
        P(None, "grp", "tile"),
        P("grp", "tile"),
        P("grp", "tile"),
        P(),
        P(("grp", "tile"), None),
        P(("grp", "tile")),
        P(("grp", "tile"), None),
        P(("grp", "tile"), None),
        P(("grp", "tile"), None),
        P(None, ("grp", "tile")),
        P(("grp", "tile")),
        P(),
        P(),
    )
    return jax.shard_map(
        functools.partial(on_device, mesh.shape["grp"], mesh.shape["tile"]),
        mesh=mesh,
        in_specs=placed,
        out_specs=(P(None, "grp", "tile"), P(None, ("grp", "tile")), P(None, "grp", "tile")),
        check_vma=False,
    )
```

```python
import functools

import jax
import jax.numpy as jnp
from jax import lax
from jax.experimental import pallas as pl
from jax.experimental.pallas import tpu as pltpu
from jax.sharding import PartitionSpec as P

MESH = pl.DeviceIdType.MESH
F32, BF16, I32 = jnp.float32, jnp.bfloat16, jnp.int32
NT = (((1,), (1,)), ((), ()))
G = 8


def iota(shape, dim):
    return lax.broadcasted_iota(I32, shape, dim)


def rows_of(row, count):
    return jnp.broadcast_to(row, (count, row.shape[1]))


def remote(src, dst, send_sem, recv_sem, device):
    return pltpu.make_async_remote_copy(
        src_ref=src,
        dst_ref=dst,
        send_sem=send_sem,
        recv_sem=recv_sem,
        device_id=device,
        device_id_type=MESH,
    )


def kernel(
    grps,
    tiles,
    atmos_in,
    kappa_in,
    sea_atm_in,
    flux_w,
    owner,
    count,
    source_in,
    dest_in,
    margin_in,
    ocean_in,
    sea_oc,
    couple,
    surf_w,
    atmos_to,
    ocean_to,
    surf_to,
    atmos,
    kappa,
    sea_atm,
    source,
    dest,
    margin,
    ocean,
    atmos_out,
    ocean_out,
    atm_surf,
    mid,
    row_send,
    row_recv,
    col_send,
    col_recv,
    src_hi,
    src_lo,
    dst_all,
    dst_send,
    dst_recv,
    dst_hi,
    weight,
    hot_src,
    hot_dst,
    table32,
    table,
    fwd_send,
    fwd_recv,
    spread,
    surf32,
    back_send,
    back_recv,
    spread2,
    total,
    summed,
    halo_ss,
    halo_rs,
    dst_ss,
    dst_rs,
    fwd_ss,
    fwd_rs,
    back_ss,
    back_rs,
    in_sem,
    out_sem,
):
    devices = grps * tiles
    groups = devices // G
    width = G * 256
    g, t = lax.axis_index("grp"), lax.axis_index("tile")
    me = g * tiles + t

    z, y, core = t // 8, lax.rem(t // 2, 4), lax.rem(t, 2)

    def peer(i, j, back=False):
        s, c = j // 2, j % 2
        dz, dy = i // 4 + s, lax.rem(i, 4) + s
        if back:
            s, dz, dy = 4 - s, 8 - dz, 8 - dy
        row = lax.rem(z + dz, 4) * 8 + lax.rem(y + dy, 4) * 2 + lax.rem(core + c, 2)
        return (lax.rem(g + s, 4), row)

    def dest_copy(i, j):
        k = i * G + j
        return remote(dst_send.at[k], dst_recv.at[k], dst_ss, dst_rs, peer(i, j))

    def fwd_copy(i, j):
        k = i * G + j
        return remote(fwd_send.at[k], fwd_recv.at[k], fwd_ss, fwd_rs.at[i], peer(i, j))

    def back_copy(i, j):
        k = i * G + j
        return remote(back_send.at[k], back_recv.at[k], back_ss, back_rs.at[i], peer(i, j, True))

    def others(i, act):
        for j in range(G):
            if j == 0:

                @pl.when(i > 0)
                def _():
                    act(i, 0)
            else:
                act(i, j)

    def settle(buffer, sem, start, size):
        part = buffer.at[pl.ds(start, size)]
        pltpu.make_async_copy(part, part, sem).wait()

    def settle_group(buffer, sems, i):
        @pl.when(i == 0)
        def _():
            settle(buffer, sems.at[0], 1, G - 1)

        @pl.when(i > 0)
        def _():
            settle(buffer, sems.at[i], i * G, G)

    barrier = pltpu.get_barrier_semaphore()

    @pl.loop(0, groups)
    def _(i):
        others(
            i,
            lambda i, j: pl.semaphore_signal(
                barrier, inc=1, device_id=peer(i, j), device_id_type=MESH
            ),
        )

    loads = {}
    for n, (name, a, b) in enumerate(
        (
            ("source", source_in, source),
            ("dest", dest_in, dest),
            ("margin", margin_in, margin),
            ("atmos", atmos_in, atmos),
            ("kappa", kappa_in, kappa),
            ("sea", sea_atm_in, sea_atm),
            ("ocean", ocean_in, ocean),
        )
    ):
        loads[name] = pltpu.make_async_copy(a, b, in_sem.at[n])
        loads[name].start()

    blocks = owner.shape[1]
    own_row = owner[...]
    own_here = jnp.broadcast_to(own_row, (blocks, blocks)).astype(F32)
    own_col = jnp.transpose(own_here)
    cnt_col = jnp.transpose(jnp.broadcast_to(count[...], (blocks, blocks)).astype(F32))
    before = iota((blocks, blocks), 0) < iota((blocks, blocks), 1)
    same = jnp.where((own_here == own_col) & before, F32(1), F32(0))
    rank = jnp.sum(same, axis=0, keepdims=True).astype(I32)
    dx = ((own_row >> 5) - g) & 3
    dz = (((own_row >> 3) & 3) - z - dx) & 3
    dy = (((own_row >> 1) & 3) - y - dx) & 3
    dc = ((own_row & 1) - core) & 1
    slot = (((dz * 4 + dy) * 4 + dx) * 2 + dc) * 2 + rank
    place = jnp.where(
        iota((2 * devices, blocks), 0) == jnp.broadcast_to(slot, (2 * devices, blocks)), F32(1), F32(0)
    ).astype(BF16)

    def placed(values):
        return jnp.dot(place, values.astype(BF16), preferred_element_type=F32)

    for name in ("source", "dest", "margin"):
        loads[name].wait()
    src = source[...]
    src_hi[...] = placed((src >> 8).astype(F32))
    src_lo[...] = placed((src & 255).astype(F32))
    dst = dest[...]
    dst_all[...] = placed((dst >> 7).astype(F32)) * 128.0 + placed((dst & 127).astype(F32))

    @pl.loop(0, devices // 4)
    def _(i):
        four = dst_all[pl.ds(pl.multiple_of(i * 8, 8), 8), :]
        for j in range(4):
            dst_send[i * 4 + j] = four[2 * j : 2 * j + 2]

    dst_recv[0] = dst_send[0]
    lanes = iota((blocks, 128), 1).astype(F32)
    live = jnp.where(lanes < cnt_col[:, :1], margin[...], F32(0))
    first = live.astype(BF16).astype(F32)
    rest = live - first
    second = rest.astype(BF16).astype(F32)
    third = rest - second
    weight[...] = placed(first) + placed(second) + placed(third)

    ids16 = (iota((16, 16, 128), 0) * 16 + iota((16, 16, 128), 1)).astype(F32).astype(BF16)
    ids8 = (iota((8, 16, 128), 0) * 16 + iota((8, 16, 128), 1)).astype(F32).astype(BF16)
    one, zero = jnp.ones((16, 128), BF16), jnp.zeros((16, 128), BF16)

    @pl.loop(0, devices // 4)
    def _(i):
        low = src_lo[pl.ds(pl.multiple_of(i * 8, 8), 8), :]
        for j in range(8):
            lo = rows_of(low[j : j + 1], 16).astype(BF16)
            hot = jnp.where(ids16 == lo[None], one[None], zero[None])
            hot_src[:, pl.ds(pl.multiple_of(i * 1024 + j * 128, 128), 128)] = hot.reshape(256, 128)

    for name in ("atmos", "kappa", "sea", "ocean"):
        loads[name].wait()
    pl.semaphore_wait(barrier, devices - 1)

    rows, cols = atmos.shape[1], atmos.shape[2]
    chans = atmos.shape[0]
    row_id, col_id = iota((rows, cols), 0), iota((rows, cols), 1)
    lane = iota((rows, 128), 1)
    beside = (
        (lax.rem(g + grps - 1, grps), t),
        (lax.rem(g + 1, grps), t),
        (g, lax.rem(t + tiles - 1, tiles)),
        (g, lax.rem(t + 1, tiles)),
    )
    edge = (g == 0, g == grps - 1, t == 0, t == tiles - 1)
    diffusion = kappa[...]
    for step in range(2):
        state = atmos if step == 0 else mid
        west = jnp.zeros((rows, 128), F32)
        east = jnp.zeros((rows, 128), F32)
        for ch in range(chans):
            x = state[ch]
            row_send[step, 0, ch : ch + 1, :] = x[0:1]
            row_send[step, 1, ch : ch + 1, :] = x[rows - 1 : rows]
            west = jnp.where(lane == ch, x[:, 0:1], west)
            east = jnp.where(lane == ch, x[:, cols - 1 : cols], east)
        col_send[step, 0] = west
        col_send[step, 1] = east
        copies = []
        for side in range(4):
            sent, got = (row_send, row_recv) if side < 2 else (col_send, col_recv)
            copies.append(
                remote(
                    sent.at[step, side % 2],
                    got.at[step, 1 - side % 2],
                    halo_ss.at[step, side],
                    halo_rs.at[step, side],
                    beside[side],
                )
            )
        for copy in copies:
            copy.start()
        if step == 0:

            @pl.loop(0, groups)
            def _(i):
                others(i, lambda i, j: dest_copy(i, j).start())

        for copy in copies:
            copy.wait()
        north = jnp.where(edge[0], F32(0), row_recv[step, 0])
        south = jnp.where(edge[1], F32(0), row_recv[step, 1])
        west = jnp.where(edge[2], F32(0), col_recv[step, 0])
        east = jnp.where(edge[3], F32(0), col_recv[step, 1])
        for ch in range(chans):
            x = state[ch]
            up = jnp.where(row_id == 0, north[ch : ch + 1], pltpu.roll(x, 1, 0))
            down = jnp.where(row_id == rows - 1, south[ch : ch + 1], pltpu.roll(x, rows - 1, 0))
            left = jnp.where(col_id == 0, west[:, ch : ch + 1], pltpu.roll(x, 1, 1))
            right = jnp.where(col_id == cols - 1, east[:, ch : ch + 1], pltpu.roll(x, cols - 1, 1))
            new = x + diffusion * (down + up + right + left - 4.0 * x)
            if step == 0:
                mid[ch] = new
            else:
                atmos_out[ch] = new

    stores = [pltpu.make_async_copy(atmos_out, atmos_to, out_sem.at[0])]
    stores[0].start()

    sea = sea_atm[...] > 0
    for f in range(12):
        mixed = flux_w[f, 0] * atmos_out[0]
        for ch in range(1, chans):
            mixed = mixed + flux_w[f, ch] * atmos_out[ch]
        flux = jnp.where(sea, jnp.tanh(mixed), F32(0))
        for half in range(2):
            part = flux[:, half * 128 : half * 128 + 128]
            if f < 8:
                table32[half, pl.ds(f, 16, stride=8), :] = part
            else:
                table32[half, pl.ds(128 + f - 8, 16, stride=4), :] = part
    for half in range(2):
        full = table32[half]
        table[:, half * 128 : half * 128 + 128] = full.astype(BF16)

    sub = iota((8, 128), 0)
    odd = jnp.where(sub >= 4, F32(1), F32(0))

    @pl.loop(0, groups)
    def _(i):
        here = pl.ds(pl.multiple_of(i * 2 * G, 2 * G), 2 * G)
        hi, w = src_hi[here, :], weight[here, :]
        for j in range(G):
            hot = hot_src[:, pl.ds(pl.multiple_of(i * width + j * 256, 256), 256)]
            found = jnp.dot(table[...], hot, preferred_element_type=F32)
            ends = []
            for part in range(2):
                mine = found[:, part * 128 : part * 128 + 128]
                h = rows_of(hi[2 * j + part : 2 * j + part + 1], 8)
                wide = mine[0:8]
                for v in range(1, 16):
                    wide = jnp.where(h == v, mine[v * 8 : v * 8 + 8], wide)
                h = h - odd
                thin = jnp.zeros((8, 128), F32)
                for v in range(8):
                    thin = jnp.where(h == 2 * v, mine[128 + v * 8 : 136 + v * 8], thin)
                scale = rows_of(w[2 * j + part : 2 * j + part + 1], 8)
                fwd_send[i * G + j, part] = (wide * scale).astype(BF16)
                ends.append((thin + pltpu.roll(thin, 4, 0)) * scale)
            fwd_send[i * G + j, 2] = jnp.where(sub < 4, ends[0], ends[1]).astype(BF16)
        others(i, lambda i, j: fwd_copy(i, j).start())

    fwd_recv[0] = fwd_send[0]

    settle(dst_recv, dst_rs, 1, devices - 1)

    @pl.loop(0, groups)
    def _(i):
        for j in range(G):
            where = dst_recv[i * G + j]
            high = jnp.floor(where * (1 / 128))
            dst_hi[i * G + j] = high
            low = where - high * 128.0
            for part in range(2):
                lo = rows_of(low[part : part + 1], 16).astype(BF16)
                hot = jnp.where(ids8 == lo[None], one[None], zero[None])
                hot_dst[:, pl.ds(pl.multiple_of(i * width + j * 256 + part * 128, 128), 128)] = hot.reshape(
                    128, 128
                )

    total[...] = jnp.zeros_like(total)

    @pl.loop(0, groups)
    def _(i):
        settle_group(fwd_recv, fwd_rs, i)
        for j in range(G):
            high = dst_hi[i * G + j]
            ends = fwd_recv[i * G + j, 2].astype(F32)
            for part in range(2):
                tile = jnp.concatenate(
                    [fwd_recv[i * G + j, part].astype(F32), pltpu.roll(ends, 4, 0) if part else ends],
                    axis=0,
                ).astype(BF16)
                hi = rows_of(high[part : part + 1], 16).astype(BF16)
                at = slice(j * 256 + part * 128, j * 256 + part * 128 + 128)
                for v in range(8):
                    spread[v * 16 : v * 16 + 16, at] = jnp.where(hi == v, tile, zero)
        total[...] += lax.dot_general(
            spread[...],
            hot_dst[:, pl.ds(pl.multiple_of(i * width, width), width)],
            NT,
            preferred_element_type=F32,
        )

    surf32[...] = jnp.zeros_like(surf32)
    for h in range(8):
        here = slice(h * 128, h * 128 + 128)
        flux = total[h * 16 : h * 16 + 16, :]
        added = couple[:, 0:1] * flux[0:1]
        for f in range(1, 12):
            added = added + couple[:, f : f + 1] * flux[f : f + 1]
        new = ocean[:, here] + jnp.where(sea_oc[:, here] > 0, added, F32(0))
        ocean_out[:, here] = new
        field = surf_w[:, 0:1] * new[0:1]
        for o in range(1, 8):
            field = field + surf_w[:, o : o + 1] * new[o : o + 1]
        surf32[h * 8 : h * 8 + 6, :] = jnp.tanh(field)
    surface = surf32[...].astype(BF16)
    stores.append(pltpu.make_async_copy(ocean_out, ocean_to, out_sem.at[1]))
    stores[1].start()

    @pl.loop(0, groups)
    def _(i):
        for j in range(G):
            k = i * G + j
            found = jnp.dot(
                surface,
                hot_dst[:, pl.ds(pl.multiple_of(i * width + j * 256, 256), 256)],
                preferred_element_type=F32,
            )
            high = dst_hi[k]
            both = []
            for part in range(2):
                mine = found[:, part * 128 : part * 128 + 128]
                h = rows_of(high[part : part + 1], 8)
                got = mine[0:8]
                for v in range(1, 8):
                    got = jnp.where(h == v, mine[v * 8 : v * 8 + 8], got)
                back_send[k, part] = got[0:4].astype(BF16)
                both.append(got)
            ends = jnp.where(sub < 2, pltpu.roll(both[0], 4, 0), pltpu.roll(both[1], 6, 0))
            back_send[k, 2] = ends[0:4].astype(BF16)
        others(i, lambda i, j: back_copy(i, j).start())

    back_recv[0] = back_send[0]

    summed[...] = jnp.zeros_like(summed)

    @pl.loop(0, groups)
    def _(i):
        settle_group(back_recv, back_rs, i)
        here = pl.ds(pl.multiple_of(i * 2 * G, 2 * G), 2 * G)
        hi, w = src_hi[here, :], weight[here, :]
        for j in range(G):
            ends = back_recv[i * G + j, 2].astype(F32)
            for part in range(2):
                most = back_recv[i * G + j, part].astype(F32)
                last = [ends[2:4], ends[0:2]] if part else [ends]
                value = jnp.concatenate([most] + last, axis=0)
                value = value * rows_of(w[2 * j + part : 2 * j + part + 1], 8)
                top = value.astype(BF16).astype(F32)
                pair = jnp.concatenate([top, value - top], axis=0).astype(BF16)
                h = rows_of(hi[2 * j + part : 2 * j + part + 1], 16).astype(BF16)
                at = slice(j * 256 + part * 128, j * 256 + part * 128 + 128)
                for v in range(16):
                    spread2[v * 16 : v * 16 + 16, at] = jnp.where(h == v, pair, zero)
        summed[...] += lax.dot_general(
            spread2[...],
            hot_src[:, pl.ds(pl.multiple_of(i * width, width), width)],
            NT,
            preferred_element_type=F32,
        )

    for half in range(2):
        here = slice(half * 128, half * 128 + 128)
        for h in range(16):
            table32[half, h * 8 : h * 8 + 8, :] = (
                summed[h * 16 : h * 16 + 8, here] + summed[h * 16 + 8 : h * 16 + 16, here]
            )
        for s in range(6):
            atm_surf[s, :, here] = jnp.where(
                sea[:, here], table32[half, pl.ds(s, 16, stride=8), :], F32(0)
            )

    stores.append(pltpu.make_async_copy(atm_surf, surf_to, out_sem.at[2]))
    stores[2].start()
    for copy in stores:
        copy.wait()

    settle(dst_send, dst_ss, 1, devices - 1)
    settle(fwd_send, fwd_ss, 1, devices - 1)
    settle(back_send, back_ss, 1, devices - 1)


def hand_over(a, b, c, a_to, b_to, c_to, sem):
    copies = [
        pltpu.make_async_copy(src, dst, sem.at[n])
        for n, (src, dst) in enumerate(((a, a_to), (b, b_to), (c, c_to)))
    ]
    for copy in copies:
        copy.start()
    for copy in copies:
        copy.wait()


def on_device(grps, tiles, *args):
    (
        atmos,
        diffusivity,
        sea_atm,
        flux_weight,
        block_owner,
        entry_count,
        source_col,
        dest_col,
        margin,
        ocean,
        sea_ocean,
        couple,
        surface_weight,
    ) = args
    devices = grps * tiles
    slots = 2 * devices
    vmem = pl.BlockSpec(memory_space=pltpu.VMEM)
    smem = pl.BlockSpec(memory_space=pltpu.SMEM)
    far = pl.BlockSpec(memory_space=pl.ANY)
    chans, rows, cols = atmos.shape
    dma = pltpu.SemaphoreType.DMA
    shapes = (
        jax.ShapeDtypeStruct(atmos.shape, F32),
        jax.ShapeDtypeStruct(ocean.shape, F32),
        jax.ShapeDtypeStruct((6, rows, cols), F32),
    )
    results = pl.pallas_call(
        functools.partial(kernel, grps, tiles),
        out_shape=shapes,
        in_specs=[far, far, far, smem, vmem, vmem, far, far, far, far, vmem, vmem, vmem],
        out_specs=(far, far, far),
        scratch_shapes=[
            pltpu.VMEM((chans, rows, cols), F32),
            pltpu.VMEM((rows, cols), F32),
            pltpu.VMEM((rows, cols), I32),
            pltpu.VMEM(source_col.shape, I32),
            pltpu.VMEM(source_col.shape, I32),
            pltpu.VMEM(source_col.shape, F32),
            pltpu.VMEM(ocean.shape, F32),
            pltpu.VMEM((chans, rows, cols), F32),
            pltpu.VMEM(ocean.shape, F32),
            pltpu.VMEM((6, rows, cols), F32),
            pltpu.VMEM((chans, rows, cols), F32),
            pltpu.VMEM((2, 2, chans, cols), F32),
            pltpu.VMEM((2, 2, chans, cols), F32),
            pltpu.VMEM((2, 2, rows, 128), F32),
            pltpu.VMEM((2, 2, rows, 128), F32),
            pltpu.VMEM((slots, 128), F32),
            pltpu.VMEM((slots, 128), F32),
            pltpu.VMEM((slots, 128), F32),
            pltpu.VMEM((devices, 2, 128), F32),
            pltpu.VMEM((devices, 2, 128), F32),
            pltpu.VMEM((devices, 2, 128), F32),
            pltpu.VMEM((slots, 128), F32),
            pltpu.VMEM((256, slots * 128), BF16),
            pltpu.VMEM((128, slots * 128), BF16),
            pltpu.VMEM((2, 192, 128), F32),
            pltpu.VMEM((192, 256), BF16),
            pltpu.VMEM((devices, 3, 8, 128), BF16),
            pltpu.VMEM((devices, 3, 8, 128), BF16),
            pltpu.VMEM((128, G * 256), BF16),
            pltpu.VMEM((64, 128), F32),
            pltpu.VMEM((devices, 3, 4, 128), BF16),
            pltpu.VMEM((devices, 3, 4, 128), BF16),
            pltpu.VMEM((256, G * 256), BF16),
            pltpu.VMEM((128, 128), F32),
            pltpu.VMEM((256, 256), F32),
            dma((2, 4)),
            dma((2, 4)),
            dma(()),
            dma(()),
            dma(()),
            dma((devices // G,)),
            dma(()),
            dma((devices // G,)),
            dma((11,)),
            dma((3,)),
        ],
        compiler_params=pltpu.CompilerParams(
            collective_id=0, has_side_effects=True, vmem_limit_bytes=56 * 1024 * 1024
        ),
    )(
        atmos,
        diffusivity,
        sea_atm,
        flux_weight,
        block_owner.reshape(1, -1),
        entry_count.reshape(1, -1),
        source_col,
        dest_col,
        margin,
        ocean,
        sea_ocean.reshape(1, -1),
        couple,
        surface_weight,
    )
    return pl.pallas_call(
        hand_over,
        out_shape=shapes,
        in_specs=[far] * 3,
        out_specs=(far, far, far),
        scratch_shapes=[dma((3,))],
    )(*results)


def solution(mesh):
    placed = (
        P(None, "grp", "tile"),
        P("grp", "tile"),
        P("grp", "tile"),
        P(),
        P(("grp", "tile"), None),
        P(("grp", "tile")),
        P(("grp", "tile"), None),
        P(("grp", "tile"), None),
        P(("grp", "tile"), None),
        P(None, ("grp", "tile")),
        P(("grp", "tile")),
        P(),
        P(),
    )
    return jax.shard_map(
        functools.partial(on_device, mesh.shape["grp"], mesh.shape["tile"]),
        mesh=mesh,
        in_specs=placed,
        out_specs=(P(None, "grp", "tile"), P(None, ("grp", "tile")), P(None, "grp", "tile")),
        check_vma=False,
    )
```

```python
import functools

import jax
import jax.numpy as jnp
from jax import lax
from jax.experimental import pallas as pl
from jax.experimental.pallas import tpu as pltpu
from jax.sharding import PartitionSpec as P

MESH = pl.DeviceIdType.MESH
F32, BF16, I32 = jnp.float32, jnp.bfloat16, jnp.int32
NT = (((1,), (1,)), ((), ()))
G = 8


def iota(shape, dim):
    return lax.broadcasted_iota(I32, shape, dim)


def rows_of(row, count):
    return jnp.broadcast_to(row, (count, row.shape[1]))


def remote(src, dst, send_sem, recv_sem, device):
    return pltpu.make_async_remote_copy(
        src_ref=src,
        dst_ref=dst,
        send_sem=send_sem,
        recv_sem=recv_sem,
        device_id=device,
        device_id_type=MESH,
    )


def kernel(
    grps,
    tiles,
    atmos_in,
    kappa_in,
    sea_atm_in,
    flux_w,
    owner,
    count,
    source_in,
    dest_in,
    margin_in,
    ocean_in,
    sea_oc,
    couple,
    surf_w,
    atmos_to,
    ocean_to,
    surf_to,
    atmos,
    kappa,
    sea_atm,
    source,
    dest,
    margin,
    ocean,
    atmos_out,
    ocean_out,
    atm_surf,
    mid,
    row_send,
    row_recv,
    col_send,
    col_recv,
    src_hi,
    src_lo,
    dst_all,
    dst_send,
    dst_recv,
    dst_hi,
    weight,
    hot_src,
    hot_dst,
    table32,
    table,
    fwd_send,
    fwd_recv,
    spread,
    surf32,
    back_send,
    back_recv,
    spread2,
    total,
    summed,
    halo_ss,
    halo_rs,
    dst_ss,
    dst_rs,
    fwd_ss,
    fwd_rs,
    back_ss,
    back_rs,
    in_sem,
    out_sem,
):
    devices = grps * tiles
    groups = devices // G
    width = G * 256
    g, t = lax.axis_index("grp"), lax.axis_index("tile")
    me = g * tiles + t

    z, y, core = t // 8, lax.rem(t // 2, 4), lax.rem(t, 2)

    def peer(i, j, back=False):
        s, c = j // 2, j % 2
        dz, dy = i // 4 + s, lax.rem(i, 4) + s
        if back:
            s, dz, dy = 4 - s, 8 - dz, 8 - dy
        row = lax.rem(z + dz, 4) * 8 + lax.rem(y + dy, 4) * 2 + lax.rem(core + c, 2)
        return (lax.rem(g + s, 4), row)

    def dest_copy(i, j):
        k = i * G + j
        return remote(dst_send.at[k], dst_recv.at[k], dst_ss, dst_rs, peer(i, j))

    def fwd_copy(i, j):
        k = i * G + j
        return remote(fwd_send.at[k], fwd_recv.at[k], fwd_ss, fwd_rs.at[i], peer(i, j))

    def back_copy(i, j):
        k = i * G + j
        return remote(back_send.at[k], back_recv.at[k], back_ss, back_rs.at[i], peer(i, j, True))

    def each_group(act):
        @pl.loop(1, groups)
        def _(i):
            act(i, 0)

        act(0, 1)

    def settle(buffer, sem, start, size):
        part = buffer.at[pl.ds(start, size)]
        pltpu.make_async_copy(part, part, sem).wait()

    def settle_group(buffer, sems, i, first):
        settle(buffer, sems.at[i], i * G + first, G - first)

    barrier = pltpu.get_barrier_semaphore()

    def greet(i, first):
        for j in range(first, G):
            pl.semaphore_signal(barrier, inc=1, device_id=peer(i, j), device_id_type=MESH)

    each_group(greet)

    loads = {}
    for n, (name, a, b) in enumerate(
        (
            ("source", source_in, source),
            ("dest", dest_in, dest),
            ("margin", margin_in, margin),
            ("atmos", atmos_in, atmos),
            ("kappa", kappa_in, kappa),
            ("sea", sea_atm_in, sea_atm),
            ("ocean", ocean_in, ocean),
        )
    ):
        loads[name] = pltpu.make_async_copy(a, b, in_sem.at[n])
        loads[name].start()

    for load in loads.values():
        load.wait()

    ids16 = (iota((16, 16, 128), 0) * 16 + iota((16, 16, 128), 1)).astype(F32).astype(BF16)
    ids8 = (iota((8, 16, 128), 0) * 16 + iota((8, 16, 128), 1)).astype(F32).astype(BF16)
    one, zero = jnp.ones((16, 128), BF16), jnp.zeros((16, 128), BF16)

    def place_blocks():
        blocks = owner.shape[1]
        own_row = owner[...]
        own_here = jnp.broadcast_to(own_row, (blocks, blocks)).astype(F32)
        own_col = jnp.transpose(own_here)
        cnt_col = jnp.transpose(jnp.broadcast_to(count[...], (blocks, blocks)).astype(F32))
        before = iota((blocks, blocks), 0) < iota((blocks, blocks), 1)
        same = jnp.where((own_here == own_col) & before, F32(1), F32(0))
        rank = jnp.sum(same, axis=0, keepdims=True).astype(I32)
        dx = ((own_row >> 5) - g) & 3
        dz = (((own_row >> 3) & 3) - z - dx) & 3
        dy = (((own_row >> 1) & 3) - y - dx) & 3
        dc = ((own_row & 1) - core) & 1
        slot = (((dz * 4 + dy) * 4 + dx) * 2 + dc) * 2 + rank
        place = jnp.where(
            iota((2 * devices, blocks), 0) == jnp.broadcast_to(slot, (2 * devices, blocks)), F32(1), F32(0)
        ).astype(BF16)

        def placed(values):
            return jnp.dot(place, values.astype(BF16), preferred_element_type=F32)

        src = source[...]
        src_hi[...] = placed((src >> 8).astype(F32))
        src_lo[...] = placed((src & 255).astype(F32))
        dst = dest[...]
        dst_all[...] = placed((dst >> 7).astype(F32)) * 128.0 + placed((dst & 127).astype(F32))

        @pl.loop(0, devices // 4)
        def _(i):
            four = dst_all[pl.ds(pl.multiple_of(i * 8, 8), 8), :]
            for j in range(4):
                dst_send[i * 4 + j] = four[2 * j : 2 * j + 2]

        dst_recv[0] = dst_send[0]
        lanes = iota((blocks, 128), 1).astype(F32)
        live = jnp.where(lanes < cnt_col[:, :1], margin[...], F32(0))
        first = live.astype(BF16).astype(F32)
        rest = live - first
        second = rest.astype(BF16).astype(F32)
        third = rest - second
        weight[...] = placed(first) + placed(second) + placed(third)

    def hot_source(i, first):
        here = pl.ds(pl.multiple_of(i * 2 * G, 2 * G), 2 * G)
        low = src_lo[here, :]
        for j in range(G):
            for part in range(2):
                lo = rows_of(low[2 * j + part : 2 * j + part + 1], 16).astype(BF16)
                hot = jnp.where(ids16 == lo[None], one[None], zero[None])
                at = pl.multiple_of(i * width + j * 256 + part * 128, 128)
                hot_src[:, pl.ds(at, 128)] = hot.reshape(256, 128)
            if j >= first:
                dest_copy(i, j).start()

    rows, cols = atmos.shape[1], atmos.shape[2]
    chans = atmos.shape[0]
    row_id, col_id = iota((rows, cols), 0), iota((rows, cols), 1)
    lane = iota((rows, 128), 1)
    beside = (
        (lax.rem(g + grps - 1, grps), t),
        (lax.rem(g + 1, grps), t),
        (g, lax.rem(t + tiles - 1, tiles)),
        (g, lax.rem(t + 1, tiles)),
    )
    edge = (g == 0, g == grps - 1, t == 0, t == tiles - 1)
    diffusion = kappa[...]
    for step in range(2):
        state = atmos if step == 0 else mid
        west = jnp.zeros((rows, 128), F32)
        east = jnp.zeros((rows, 128), F32)
        for ch in range(chans):
            x = state[ch]
            row_send[step, 0, ch : ch + 1, :] = x[0:1]
            row_send[step, 1, ch : ch + 1, :] = x[rows - 1 : rows]
            west = jnp.where(lane == ch, x[:, 0:1], west)
            east = jnp.where(lane == ch, x[:, cols - 1 : cols], east)
        col_send[step, 0] = west
        col_send[step, 1] = east
        copies = []
        for side in range(4):
            sent, got = (row_send, row_recv) if side < 2 else (col_send, col_recv)
            copies.append(
                remote(
                    sent.at[step, side % 2],
                    got.at[step, 1 - side % 2],
                    halo_ss.at[step, side],
                    halo_rs.at[step, side],
                    beside[side],
                )
            )
        if step == 0:
            pl.semaphore_wait(barrier, devices - 1)
        for copy in copies:
            copy.start()
        if step == 0:
            place_blocks()

            @pl.loop(1, groups // 2)
            def _(i):
                hot_source(i, 0)

            hot_source(0, 1)
        else:

            @pl.loop(groups // 2, groups)
            def _(i):
                hot_source(i, 0)

        for copy in copies:
            copy.wait()
        north = jnp.where(edge[0], F32(0), row_recv[step, 0])
        south = jnp.where(edge[1], F32(0), row_recv[step, 1])
        west = jnp.where(edge[2], F32(0), col_recv[step, 0])
        east = jnp.where(edge[3], F32(0), col_recv[step, 1])
        for ch in range(chans):
            x = state[ch]
            up = jnp.where(row_id == 0, north[ch : ch + 1], pltpu.roll(x, 1, 0))
            down = jnp.where(row_id == rows - 1, south[ch : ch + 1], pltpu.roll(x, rows - 1, 0))
            left = jnp.where(col_id == 0, west[:, ch : ch + 1], pltpu.roll(x, 1, 1))
            right = jnp.where(col_id == cols - 1, east[:, ch : ch + 1], pltpu.roll(x, cols - 1, 1))
            new = x + diffusion * (down + up + right + left - 4.0 * x)
            if step == 0:
                mid[ch] = new
            else:
                atmos_out[ch] = new

    stores = [pltpu.make_async_copy(atmos_out, atmos_to, out_sem.at[0])]
    stores[0].start()

    sea = sea_atm[...] > 0
    for f in range(12):
        mixed = flux_w[f, 0] * atmos_out[0]
        for ch in range(1, chans):
            mixed = mixed + flux_w[f, ch] * atmos_out[ch]
        flux = jnp.where(sea, jnp.tanh(mixed), F32(0))
        for half in range(2):
            part = flux[:, half * 128 : half * 128 + 128]
            if f < 8:
                table32[half, pl.ds(f, 16, stride=8), :] = part
            else:
                table32[half, pl.ds(128 + f - 8, 16, stride=4), :] = part
    for half in range(2):
        full = table32[half]
        table[:, half * 128 : half * 128 + 128] = full.astype(BF16)

    sub = iota((8, 128), 0)
    odd = jnp.where(sub >= 4, F32(1), F32(0))

    def give(i, first):
        here = pl.ds(pl.multiple_of(i * 2 * G, 2 * G), 2 * G)
        hi, w = src_hi[here, :], weight[here, :]
        for j in range(G):
            hot = hot_src[:, pl.ds(pl.multiple_of(i * width + j * 256, 256), 256)]
            found = jnp.dot(table[...], hot, preferred_element_type=F32)
            ends = []
            for part in range(2):
                mine = found[:, part * 128 : part * 128 + 128]
                h = rows_of(hi[2 * j + part : 2 * j + part + 1], 8)
                wide = mine[0:8]
                for v in range(1, 16):
                    wide = jnp.where(h == v, mine[v * 8 : v * 8 + 8], wide)
                h = h - odd
                thin = jnp.zeros((8, 128), F32)
                for v in range(8):
                    thin = jnp.where(h == 2 * v, mine[128 + v * 8 : 136 + v * 8], thin)
                scale = rows_of(w[2 * j + part : 2 * j + part + 1], 8)
                fwd_send[i * G + j, part] = (wide * scale).astype(BF16)
                ends.append((thin + pltpu.roll(thin, 4, 0)) * scale)
            fwd_send[i * G + j, 2] = jnp.where(sub < 4, ends[0], ends[1]).astype(BF16)
            if j >= first:
                fwd_copy(i, j).start()

    each_group(give)

    fwd_recv[0] = fwd_send[0]

    settle(dst_recv, dst_rs, 1, devices - 1)

    @pl.loop(0, groups)
    def _(i):
        for j in range(G):
            where = dst_recv[i * G + j]
            high = jnp.floor(where * (1 / 128))
            dst_hi[i * G + j] = high
            low = where - high * 128.0
            for part in range(2):
                lo = rows_of(low[part : part + 1], 16).astype(BF16)
                hot = jnp.where(ids8 == lo[None], one[None], zero[None])
                hot_dst[:, pl.ds(pl.multiple_of(i * width + j * 256 + part * 128, 128), 128)] = hot.reshape(
                    128, 128
                )

    total[...] = jnp.zeros_like(total)

    def collect(i, first):
        settle_group(fwd_recv, fwd_rs, i, first)
        for j in range(G):
            high = dst_hi[i * G + j]
            ends = fwd_recv[i * G + j, 2].astype(F32)
            for part in range(2):
                tile = jnp.concatenate(
                    [fwd_recv[i * G + j, part].astype(F32), pltpu.roll(ends, 4, 0) if part else ends],
                    axis=0,
                ).astype(BF16)
                hi = rows_of(high[part : part + 1], 16).astype(BF16)
                at = slice(j * 256 + part * 128, j * 256 + part * 128 + 128)
                for v in range(8):
                    spread[v * 16 : v * 16 + 16, at] = jnp.where(hi == v, tile, zero)
        total[...] += lax.dot_general(
            spread[...],
            hot_dst[:, pl.ds(pl.multiple_of(i * width, width), width)],
            NT,
            preferred_element_type=F32,
        )

    each_group(collect)

    surf32[...] = jnp.zeros_like(surf32)
    for h in range(8):
        here = slice(h * 128, h * 128 + 128)
        flux = total[h * 16 : h * 16 + 16, :]
        added = couple[:, 0:1] * flux[0:1]
        for f in range(1, 12):
            added = added + couple[:, f : f + 1] * flux[f : f + 1]
        new = ocean[:, here] + jnp.where(sea_oc[:, here] > 0, added, F32(0))
        ocean_out[:, here] = new
        field = surf_w[:, 0:1] * new[0:1]
        for o in range(1, 8):
            field = field + surf_w[:, o : o + 1] * new[o : o + 1]
        surf32[h * 8 : h * 8 + 6, :] = jnp.tanh(field)
    surface = surf32[...].astype(BF16)
    stores.append(pltpu.make_async_copy(ocean_out, ocean_to, out_sem.at[1]))
    stores[1].start()

    def answer(i, first):
        for j in range(G):
            k = i * G + j
            found = jnp.dot(
                surface,
                hot_dst[:, pl.ds(pl.multiple_of(i * width + j * 256, 256), 256)],
                preferred_element_type=F32,
            )
            high = dst_hi[k]
            both = []
            for part in range(2):
                mine = found[:, part * 128 : part * 128 + 128]
                h = rows_of(high[part : part + 1], 8)
                got = mine[0:8]
                for v in range(1, 8):
                    got = jnp.where(h == v, mine[v * 8 : v * 8 + 8], got)
                back_send[k, part] = got[0:4].astype(BF16)
                both.append(got)
            ends = jnp.where(sub < 2, pltpu.roll(both[0], 4, 0), pltpu.roll(both[1], 6, 0))
            back_send[k, 2] = ends[0:4].astype(BF16)
            if j >= first:
                back_copy(i, j).start()

    each_group(answer)

    back_recv[0] = back_send[0]

    summed[...] = jnp.zeros_like(summed)

    def gather_up(i, first):
        settle_group(back_recv, back_rs, i, first)
        here = pl.ds(pl.multiple_of(i * 2 * G, 2 * G), 2 * G)
        hi, w = src_hi[here, :], weight[here, :]
        for j in range(G):
            ends = back_recv[i * G + j, 2].astype(F32)
            for part in range(2):
                most = back_recv[i * G + j, part].astype(F32)
                last = [ends[2:4], ends[0:2]] if part else [ends]
                value = jnp.concatenate([most] + last, axis=0)
                value = value * rows_of(w[2 * j + part : 2 * j + part + 1], 8)
                pair = jnp.concatenate([value, value], axis=0).astype(BF16)
                h = (rows_of(hi[2 * j + part : 2 * j + part + 1], 16) - upper).astype(BF16)
                at = slice(j * 256 + part * 128, j * 256 + part * 128 + 128)
                for v in range(8):
                    spread2[v * 16 : v * 16 + 16, at] = jnp.where(h == 2 * v, pair, zero)
        added = lax.dot_general(
            spread2[...],
            hot_src[:, pl.ds(pl.multiple_of(i * width, width), width)],
            NT,
            preferred_element_type=F32,
        )
        summed[0] += added[:, 0:128]
        summed[1] += added[:, 128:256]

    upper = jnp.where(iota((16, 128), 0) >= 8, F32(1), F32(0))
    each_group(gather_up)

    for half in range(2):
        here = slice(half * 128, half * 128 + 128)
        for s in range(6):
            atm_surf[s, :, here] = jnp.where(
                sea[:, here], summed[half, pl.ds(s, 16, stride=8), :], F32(0)
            )

    stores.append(pltpu.make_async_copy(atm_surf, surf_to, out_sem.at[2]))
    stores[2].start()
    for copy in stores:
        copy.wait()

    settle(dst_send, dst_ss, 1, devices - 1)
    settle(fwd_send, fwd_ss, 1, devices - 1)
    settle(back_send, back_ss, 1, devices - 1)


def hand_over(a, b, c, a_to, b_to, c_to, a_here, b_here, c_here, sem):
    here = (a_here.at[pl.ds(0, 8)], a_here.at[pl.ds(8, 8)], b_here, c_here)
    into = (a.at[pl.ds(0, 8)], a.at[pl.ds(8, 8)], b, c)
    out = (a_to.at[pl.ds(0, 8)], a_to.at[pl.ds(8, 8)], b_to, c_to)
    loads = [pltpu.make_async_copy(into[n], here[n], sem.at[n]) for n in range(4)]
    stores = [pltpu.make_async_copy(here[n], out[n], sem.at[4 + n]) for n in range(4)]
    for copy in loads:
        copy.start()
    for n in range(4):
        loads[n].wait()
        stores[n].start()
    for copy in stores:
        copy.wait()


def on_device(grps, tiles, *args):
    (
        atmos,
        diffusivity,
        sea_atm,
        flux_weight,
        block_owner,
        entry_count,
        source_col,
        dest_col,
        margin,
        ocean,
        sea_ocean,
        couple,
        surface_weight,
    ) = args
    devices = grps * tiles
    slots = 2 * devices
    vmem = pl.BlockSpec(memory_space=pltpu.VMEM)
    smem = pl.BlockSpec(memory_space=pltpu.SMEM)
    far = pl.BlockSpec(memory_space=pl.ANY)
    chans, rows, cols = atmos.shape
    dma = pltpu.SemaphoreType.DMA
    shapes = (
        jax.ShapeDtypeStruct(atmos.shape, F32),
        jax.ShapeDtypeStruct(ocean.shape, F32),
        jax.ShapeDtypeStruct((6, rows, cols), F32),
    )
    results = pl.pallas_call(
        functools.partial(kernel, grps, tiles),
        out_shape=shapes,
        in_specs=[far, far, far, smem, vmem, vmem, far, far, far, far, vmem, vmem, vmem],
        out_specs=(far, far, far),
        scratch_shapes=[
            pltpu.VMEM((chans, rows, cols), F32),
            pltpu.VMEM((rows, cols), F32),
            pltpu.VMEM((rows, cols), I32),
            pltpu.VMEM(source_col.shape, I32),
            pltpu.VMEM(source_col.shape, I32),
            pltpu.VMEM(source_col.shape, F32),
            pltpu.VMEM(ocean.shape, F32),
            pltpu.VMEM((chans, rows, cols), F32),
            pltpu.VMEM(ocean.shape, F32),
            pltpu.VMEM((6, rows, cols), F32),
            pltpu.VMEM((chans, rows, cols), F32),
            pltpu.VMEM((2, 2, chans, cols), F32),
            pltpu.VMEM((2, 2, chans, cols), F32),
            pltpu.VMEM((2, 2, rows, 128), F32),
            pltpu.VMEM((2, 2, rows, 128), F32),
            pltpu.VMEM((slots, 128), F32),
            pltpu.VMEM((slots, 128), F32),
            pltpu.VMEM((slots, 128), F32),
            pltpu.VMEM((devices, 2, 128), F32),
            pltpu.VMEM((devices, 2, 128), F32),
            pltpu.VMEM((devices, 2, 128), F32),
            pltpu.VMEM((slots, 128), F32),
            pltpu.VMEM((256, slots * 128), BF16),
            pltpu.VMEM((128, slots * 128), BF16),
            pltpu.VMEM((2, 192, 128), F32),
            pltpu.VMEM((192, 256), BF16),
            pltpu.VMEM((devices, 3, 8, 128), BF16),
            pltpu.VMEM((devices, 3, 8, 128), BF16),
            pltpu.VMEM((128, G * 256), BF16),
            pltpu.VMEM((64, 128), F32),
            pltpu.VMEM((devices, 3, 4, 128), BF16),
            pltpu.VMEM((devices, 3, 4, 128), BF16),
            pltpu.VMEM((128, G * 256), BF16),
            pltpu.VMEM((128, 128), F32),
            pltpu.VMEM((2, 128, 128), F32),
            dma((2, 4)),
            dma((2, 4)),
            dma(()),
            dma(()),
            dma(()),
            dma((devices // G,)),
            dma(()),
            dma((devices // G,)),
            dma((11,)),
            dma((3,)),
        ],
        compiler_params=pltpu.CompilerParams(
            collective_id=0, has_side_effects=True, vmem_limit_bytes=56 * 1024 * 1024
        ),
    )(
        atmos,
        diffusivity,
        sea_atm,
        flux_weight,
        block_owner.reshape(1, -1),
        entry_count.reshape(1, -1),
        source_col,
        dest_col,
        margin,
        ocean,
        sea_ocean.reshape(1, -1),
        couple,
        surface_weight,
    )
    return pl.pallas_call(
        hand_over,
        out_shape=shapes,
        in_specs=[far] * 3,
        out_specs=(far, far, far),
        scratch_shapes=[pltpu.VMEM(x.shape, F32) for x in shapes] + [dma((8,))],
    )(*results)


def solution(mesh):
    placed = (
        P(None, "grp", "tile"),
        P("grp", "tile"),
        P("grp", "tile"),
        P(),
        P(("grp", "tile"), None),
        P(("grp", "tile")),
        P(("grp", "tile"), None),
        P(("grp", "tile"), None),
        P(("grp", "tile"), None),
        P(None, ("grp", "tile")),
        P(("grp", "tile")),
        P(),
        P(),
    )
    return jax.shard_map(
        functools.partial(on_device, mesh.shape["grp"], mesh.shape["tile"]),
        mesh=mesh,
        in_specs=placed,
        out_specs=(P(None, "grp", "tile"), P(None, ("grp", "tile")), P(None, "grp", "tile")),
        check_vma=False,
    )
```

```python
import functools

import jax
import jax.numpy as jnp
from jax import lax
from jax.experimental import pallas as pl
from jax.experimental.pallas import tpu as pltpu
from jax.sharding import PartitionSpec as P

MESH = pl.DeviceIdType.MESH
F32, BF16, I32 = jnp.float32, jnp.bfloat16, jnp.int32
NT = (((1,), (1,)), ((), ()))
G = 8


def iota(shape, dim):
    return lax.broadcasted_iota(I32, shape, dim)


def rows_of(row, count):
    return jnp.broadcast_to(row, (count, row.shape[1]))


def remote(src, dst, send_sem, recv_sem, device):
    return pltpu.make_async_remote_copy(
        src_ref=src,
        dst_ref=dst,
        send_sem=send_sem,
        recv_sem=recv_sem,
        device_id=device,
        device_id_type=MESH,
    )


def kernel(
    grps,
    tiles,
    atmos_in,
    kappa_in,
    sea_atm_in,
    flux_w,
    owner,
    count,
    source_in,
    dest_in,
    margin_in,
    ocean_in,
    sea_oc,
    couple,
    surf_w,
    atmos_to,
    ocean_to,
    surf_to,
    atmos,
    kappa,
    sea_atm,
    source,
    dest,
    margin,
    ocean,
    atmos_out,
    ocean_out,
    atm_surf,
    mid,
    row_send,
    row_recv,
    col_send,
    col_recv,
    src_hi,
    src_lo,
    dst_all,
    dst_send,
    dst_recv,
    dst_hi,
    weight,
    hot_src,
    hot_dst,
    table32,
    table,
    fwd_send,
    fwd_recv,
    spread,
    surf32,
    back_send,
    back_recv,
    spread2,
    total,
    summed,
    halo_ss,
    halo_rs,
    dst_ss,
    dst_rs,
    fwd_ss,
    fwd_rs,
    back_ss,
    back_rs,
    in_sem,
    out_sem,
):
    devices = grps * tiles
    groups = devices // G
    width = G * 256
    g, t = lax.axis_index("grp"), lax.axis_index("tile")
    me = g * tiles + t

    z, y, core = t // 8, lax.rem(t // 2, 4), lax.rem(t, 2)

    def peer(i, j, back=False):
        s, c = j // 2, j % 2
        dz, dy = i // 4 + s, lax.rem(i, 4) + s
        if back:
            s, dz, dy = 4 - s, 8 - dz, 8 - dy
        row = lax.rem(z + dz, 4) * 8 + lax.rem(y + dy, 4) * 2 + lax.rem(core + c, 2)
        return (lax.rem(g + s, 4), row)

    def dest_copy(i, j):
        k = i * G + j
        return remote(dst_send.at[k], dst_recv.at[k], dst_ss, dst_rs, peer(i, j))

    def fwd_copy(i, j):
        k = i * G + j
        return remote(fwd_send.at[k], fwd_recv.at[k], fwd_ss, fwd_rs.at[i], peer(i, j))

    def back_copy(i, j):
        k = i * G + j
        return remote(back_send.at[k], back_recv.at[k], back_ss, back_rs.at[i], peer(i, j, True))

    def each_group(act):
        @pl.loop(1, groups)
        def _(i):
            act(i, 0)

        act(0, 1)

    def start_all(make):
        def act(i, first):
            for j in range(first, G):
                make(i, j).start()

        return act

    def settle(buffer, sem, start, size):
        part = buffer.at[pl.ds(start, size)]
        pltpu.make_async_copy(part, part, sem).wait()

    def settle_group(buffer, sems, i, first):
        settle(buffer, sems.at[i], i * G + first, G - first)

    barrier = pltpu.get_barrier_semaphore()

    def greet(i, first):
        for j in range(first, G):
            pl.semaphore_signal(barrier, inc=1, device_id=peer(i, j), device_id_type=MESH)

    each_group(greet)

    loads = {}
    for n, (name, a, b) in enumerate(
        (
            ("source", source_in, source),
            ("dest", dest_in, dest),
            ("margin", margin_in, margin),
            ("atmos", atmos_in, atmos),
            ("kappa", kappa_in, kappa),
            ("sea", sea_atm_in, sea_atm),
            ("ocean", ocean_in, ocean),
        )
    ):
        loads[name] = pltpu.make_async_copy(a, b, in_sem.at[n])
        loads[name].start()

    for load in loads.values():
        load.wait()

    ids16 = (iota((16, 16, 128), 0) * 16 + iota((16, 16, 128), 1)).astype(F32).astype(BF16)
    ids8 = (iota((8, 16, 128), 0) * 16 + iota((8, 16, 128), 1)).astype(F32).astype(BF16)
    one, zero = jnp.ones((16, 128), BF16), jnp.zeros((16, 128), BF16)

    def place_blocks():
        blocks = owner.shape[1]
        own_row = owner[...]
        own_here = jnp.broadcast_to(own_row, (blocks, blocks)).astype(F32)
        own_col = jnp.transpose(own_here)
        cnt_col = jnp.transpose(jnp.broadcast_to(count[...], (blocks, blocks)).astype(F32))
        before = iota((blocks, blocks), 0) < iota((blocks, blocks), 1)
        same = jnp.where((own_here == own_col) & before, F32(1), F32(0))
        rank = jnp.sum(same, axis=0, keepdims=True).astype(I32)
        dx = ((own_row >> 5) - g) & 3
        dz = (((own_row >> 3) & 3) - z - dx) & 3
        dy = (((own_row >> 1) & 3) - y - dx) & 3
        dc = ((own_row & 1) - core) & 1
        slot = (((dz * 4 + dy) * 4 + dx) * 2 + dc) * 2 + rank
        place = jnp.where(
            iota((2 * devices, blocks), 0) == jnp.broadcast_to(slot, (2 * devices, blocks)), F32(1), F32(0)
        ).astype(BF16)

        def placed(values):
            return jnp.dot(place, values.astype(BF16), preferred_element_type=F32)

        src = source[...]
        src_hi[...] = placed((src >> 8).astype(F32))
        src_lo[...] = placed((src & 255).astype(F32))
        dst = dest[...]
        dst_all[...] = placed((dst >> 7).astype(F32)) * 128.0 + placed((dst & 127).astype(F32))

        @pl.loop(0, devices // 4)
        def _(i):
            four = dst_all[pl.ds(pl.multiple_of(i * 8, 8), 8), :]
            for j in range(4):
                dst_send[i * 4 + j] = four[2 * j : 2 * j + 2]

        dst_recv[0] = dst_send[0]
        lanes = iota((blocks, 128), 1).astype(F32)
        live = jnp.where(lanes < cnt_col[:, :1], margin[...], F32(0))
        first = live.astype(BF16).astype(F32)
        rest = live - first
        second = rest.astype(BF16).astype(F32)
        third = rest - second
        weight[...] = placed(first) + placed(second) + placed(third)

    def hot_source(i):
        here = pl.ds(pl.multiple_of(i * 2 * G, 2 * G), 2 * G)
        low = src_lo[here, :]
        for j in range(G):
            for part in range(2):
                lo = rows_of(low[2 * j + part : 2 * j + part + 1], 16).astype(BF16)
                hot = jnp.where(ids16 == lo[None], one[None], zero[None])
                at = pl.multiple_of(i * width + j * 256 + part * 128, 128)
                hot_src[:, pl.ds(at, 128)] = hot.reshape(256, 128)

    rows, cols = atmos.shape[1], atmos.shape[2]
    chans = atmos.shape[0]
    row_id, col_id = iota((rows, cols), 0), iota((rows, cols), 1)
    lane = iota((rows, 128), 1)
    beside = (
        (lax.rem(g + grps - 1, grps), t),
        (lax.rem(g + 1, grps), t),
        (g, lax.rem(t + tiles - 1, tiles)),
        (g, lax.rem(t + 1, tiles)),
    )
    edge = (g == 0, g == grps - 1, t == 0, t == tiles - 1)
    diffusion = kappa[...]
    for step in range(2):
        state = atmos if step == 0 else mid
        west = jnp.zeros((rows, 128), F32)
        east = jnp.zeros((rows, 128), F32)
        for ch in range(chans):
            x = state[ch]
            row_send[step, 0, ch : ch + 1, :] = x[0:1]
            row_send[step, 1, ch : ch + 1, :] = x[rows - 1 : rows]
            west = jnp.where(lane == ch, x[:, 0:1], west)
            east = jnp.where(lane == ch, x[:, cols - 1 : cols], east)
        col_send[step, 0] = west
        col_send[step, 1] = east
        copies = []
        for side in range(4):
            sent, got = (row_send, row_recv) if side < 2 else (col_send, col_recv)
            copies.append(
                remote(
                    sent.at[step, side % 2],
                    got.at[step, 1 - side % 2],
                    halo_ss.at[step, side],
                    halo_rs.at[step, side],
                    beside[side],
                )
            )
        if step == 0:
            pl.semaphore_wait(barrier, devices - 1)
        for copy in copies:
            copy.start()
        if step == 0:
            place_blocks()
            each_group(start_all(dest_copy))
        else:

            @pl.loop(0, groups)
            def _(i):
                hot_source(i)

        for copy in copies:
            copy.wait()
        north = jnp.where(edge[0], F32(0), row_recv[step, 0])
        south = jnp.where(edge[1], F32(0), row_recv[step, 1])
        west = jnp.where(edge[2], F32(0), col_recv[step, 0])
        east = jnp.where(edge[3], F32(0), col_recv[step, 1])
        for ch in range(chans):
            x = state[ch]
            up = jnp.where(row_id == 0, north[ch : ch + 1], pltpu.roll(x, 1, 0))
            down = jnp.where(row_id == rows - 1, south[ch : ch + 1], pltpu.roll(x, rows - 1, 0))
            left = jnp.where(col_id == 0, west[:, ch : ch + 1], pltpu.roll(x, 1, 1))
            right = jnp.where(col_id == cols - 1, east[:, ch : ch + 1], pltpu.roll(x, cols - 1, 1))
            new = x + diffusion * (down + up + right + left - 4.0 * x)
            if step == 0:
                mid[ch] = new
            else:
                atmos_out[ch] = new

    stores = [pltpu.make_async_copy(atmos_out, atmos_to, out_sem.at[0])]
    stores[0].start()

    sea = sea_atm[...] > 0
    for f in range(12):
        mixed = flux_w[f, 0] * atmos_out[0]
        for ch in range(1, chans):
            mixed = mixed + flux_w[f, ch] * atmos_out[ch]
        flux = jnp.where(sea, jnp.tanh(mixed), F32(0))
        for half in range(2):
            part = flux[:, half * 128 : half * 128 + 128]
            if f < 8:
                table32[half, pl.ds(f, 16, stride=8), :] = part
            else:
                table32[half, pl.ds(128 + f - 8, 16, stride=4), :] = part
    for half in range(2):
        full = table32[half]
        table[:, half * 128 : half * 128 + 128] = full.astype(BF16)

    sub = iota((8, 128), 0)
    odd = jnp.where(sub >= 4, F32(1), F32(0))

    def give(i, first):
        here = pl.ds(pl.multiple_of(i * 2 * G, 2 * G), 2 * G)
        hi, w = src_hi[here, :], weight[here, :]
        for j in range(G):
            hot = hot_src[:, pl.ds(pl.multiple_of(i * width + j * 256, 256), 256)]
            found = jnp.dot(table[...], hot, preferred_element_type=F32)
            ends = []
            for part in range(2):
                mine = found[:, part * 128 : part * 128 + 128]
                h = rows_of(hi[2 * j + part : 2 * j + part + 1], 8)
                wide = mine[0:8]
                for v in range(1, 16):
                    wide = jnp.where(h == v, mine[v * 8 : v * 8 + 8], wide)
                h = h - odd
                thin = jnp.zeros((8, 128), F32)
                for v in range(8):
                    thin = jnp.where(h == 2 * v, mine[128 + v * 8 : 136 + v * 8], thin)
                scale = rows_of(w[2 * j + part : 2 * j + part + 1], 8)
                fwd_send[i * G + j, part] = (wide * scale).astype(BF16)
                ends.append((thin + pltpu.roll(thin, 4, 0)) * scale)
            fwd_send[i * G + j, 2] = jnp.where(sub < 4, ends[0], ends[1]).astype(BF16)
        start_all(fwd_copy)(i, first)

    each_group(give)

    fwd_recv[0] = fwd_send[0]

    settle(dst_recv, dst_rs, 1, devices - 1)

    @pl.loop(0, groups)
    def _(i):
        for j in range(G):
            where = dst_recv[i * G + j]
            high = jnp.floor(where * (1 / 128))
            dst_hi[i * G + j] = high
            low = where - high * 128.0
            for part in range(2):
                lo = rows_of(low[part : part + 1], 16).astype(BF16)
                hot = jnp.where(ids8 == lo[None], one[None], zero[None])
                hot_dst[:, pl.ds(pl.multiple_of(i * width + j * 256 + part * 128, 128), 128)] = hot.reshape(
                    128, 128
                )

    total[...] = jnp.zeros_like(total)

    def collect(i, first):
        settle_group(fwd_recv, fwd_rs, i, first)
        for j in range(G):
            high = dst_hi[i * G + j]
            ends = fwd_recv[i * G + j, 2].astype(F32)
            for part in range(2):
                tile = jnp.concatenate(
                    [fwd_recv[i * G + j, part].astype(F32), pltpu.roll(ends, 4, 0) if part else ends],
                    axis=0,
                ).astype(BF16)
                hi = rows_of(high[part : part + 1], 16).astype(BF16)
                at = slice(j * 256 + part * 128, j * 256 + part * 128 + 128)
                for v in range(8):
                    spread[v * 16 : v * 16 + 16, at] = jnp.where(hi == v, tile, zero)
        total[...] += lax.dot_general(
            spread[...],
            hot_dst[:, pl.ds(pl.multiple_of(i * width, width), width)],
            NT,
            preferred_element_type=F32,
        )

    each_group(collect)

    surf32[...] = jnp.zeros_like(surf32)
    for h in range(8):
        here = slice(h * 128, h * 128 + 128)
        flux = total[h * 16 : h * 16 + 16, :]
        added = couple[:, 0:1] * flux[0:1]
        for f in range(1, 12):
            added = added + couple[:, f : f + 1] * flux[f : f + 1]
        new = ocean[:, here] + jnp.where(sea_oc[:, here] > 0, added, F32(0))
        ocean_out[:, here] = new
        field = surf_w[:, 0:1] * new[0:1]
        for o in range(1, 8):
            field = field + surf_w[:, o : o + 1] * new[o : o + 1]
        surf32[h * 8 : h * 8 + 6, :] = jnp.tanh(field)
    surface = surf32[...].astype(BF16)
    stores.append(pltpu.make_async_copy(ocean_out, ocean_to, out_sem.at[1]))
    stores[1].start()

    def answer(i, first):
        for j in range(G):
            k = i * G + j
            found = jnp.dot(
                surface,
                hot_dst[:, pl.ds(pl.multiple_of(i * width + j * 256, 256), 256)],
                preferred_element_type=F32,
            )
            high = dst_hi[k]
            both = []
            for part in range(2):
                mine = found[:, part * 128 : part * 128 + 128]
                h = rows_of(high[part : part + 1], 8)
                got = mine[0:8]
                for v in range(1, 8):
                    got = jnp.where(h == v, mine[v * 8 : v * 8 + 8], got)
                back_send[k, part] = got[0:4].astype(BF16)
                both.append(got)
            ends = jnp.where(sub < 2, pltpu.roll(both[0], 4, 0), pltpu.roll(both[1], 6, 0))
            back_send[k, 2] = ends[0:4].astype(BF16)
        start_all(back_copy)(i, first)

    each_group(answer)

    back_recv[0] = back_send[0]

    summed[...] = jnp.zeros_like(summed)

    def gather_up(i, first):
        settle_group(back_recv, back_rs, i, first)
        here = pl.ds(pl.multiple_of(i * 2 * G, 2 * G), 2 * G)
        hi, w = src_hi[here, :], weight[here, :]
        for j in range(G):
            ends = back_recv[i * G + j, 2].astype(F32)
            for part in range(2):
                most = back_recv[i * G + j, part].astype(F32)
                last = [ends[2:4], ends[0:2]] if part else [ends]
                value = jnp.concatenate([most] + last, axis=0)
                value = value * rows_of(w[2 * j + part : 2 * j + part + 1], 8)
                top = value.astype(BF16).astype(F32)
                pair = jnp.concatenate([top, value - top], axis=0).astype(BF16)
                h = rows_of(hi[2 * j + part : 2 * j + part + 1], 16).astype(BF16)
                at = slice(j * 256 + part * 128, j * 256 + part * 128 + 128)
                for v in range(16):
                    spread2[v * 16 : v * 16 + 16, at] = jnp.where(h == v, pair, zero)
        added = lax.dot_general(
            spread2[...],
            hot_src[:, pl.ds(pl.multiple_of(i * width, width), width)],
            NT,
            preferred_element_type=F32,
        )
        summed[...] += added

    each_group(gather_up)

    for half in range(2):
        here = slice(half * 128, half * 128 + 128)
        for h in range(16):
            table32[half, h * 8 : h * 8 + 8, :] = (
                summed[h * 16 : h * 16 + 8, here] + summed[h * 16 + 8 : h * 16 + 16, here]
            )
        for s in range(6):
            atm_surf[s, :, here] = jnp.where(
                sea[:, here], table32[half, pl.ds(s, 16, stride=8), :], F32(0)
            )

    stores.append(pltpu.make_async_copy(atm_surf, surf_to, out_sem.at[2]))
    stores[2].start()
    for copy in stores:
        copy.wait()

    settle(dst_send, dst_ss, 1, devices - 1)
    settle(fwd_send, fwd_ss, 1, devices - 1)
    settle(back_send, back_ss, 1, devices - 1)


def hand_over(a, b, c, a_to, b_to, c_to, a_here, b_here, c_here, sem):
    here = (a_here.at[pl.ds(0, 8)], a_here.at[pl.ds(8, 8)], b_here, c_here)
    into = (a.at[pl.ds(0, 8)], a.at[pl.ds(8, 8)], b, c)
    out = (a_to.at[pl.ds(0, 8)], a_to.at[pl.ds(8, 8)], b_to, c_to)
    loads = [pltpu.make_async_copy(into[n], here[n], sem.at[n]) for n in range(4)]
    stores = [pltpu.make_async_copy(here[n], out[n], sem.at[4 + n]) for n in range(4)]
    for copy in loads:
        copy.start()
    for n in range(4):
        loads[n].wait()
        stores[n].start()
    for copy in stores:
        copy.wait()


def on_device(grps, tiles, *args):
    (
        atmos,
        diffusivity,
        sea_atm,
        flux_weight,
        block_owner,
        entry_count,
        source_col,
        dest_col,
        margin,
        ocean,
        sea_ocean,
        couple,
        surface_weight,
    ) = args
    devices = grps * tiles
    slots = 2 * devices
    vmem = pl.BlockSpec(memory_space=pltpu.VMEM)
    smem = pl.BlockSpec(memory_space=pltpu.SMEM)
    far = pl.BlockSpec(memory_space=pl.ANY)
    chans, rows, cols = atmos.shape
    dma = pltpu.SemaphoreType.DMA
    shapes = (
        jax.ShapeDtypeStruct(atmos.shape, F32),
        jax.ShapeDtypeStruct(ocean.shape, F32),
        jax.ShapeDtypeStruct((6, rows, cols), F32),
    )
    results = pl.pallas_call(
        functools.partial(kernel, grps, tiles),
        out_shape=shapes,
        in_specs=[far, far, far, smem, vmem, vmem, far, far, far, far, vmem, vmem, vmem],
        out_specs=(far, far, far),
        scratch_shapes=[
            pltpu.VMEM((chans, rows, cols), F32),
            pltpu.VMEM((rows, cols), F32),
            pltpu.VMEM((rows, cols), I32),
            pltpu.VMEM(source_col.shape, I32),
            pltpu.VMEM(source_col.shape, I32),
            pltpu.VMEM(source_col.shape, F32),
            pltpu.VMEM(ocean.shape, F32),
            pltpu.VMEM((chans, rows, cols), F32),
            pltpu.VMEM(ocean.shape, F32),
            pltpu.VMEM((6, rows, cols), F32),
            pltpu.VMEM((chans, rows, cols), F32),
            pltpu.VMEM((2, 2, chans, cols), F32),
            pltpu.VMEM((2, 2, chans, cols), F32),
            pltpu.VMEM((2, 2, rows, 128), F32),
            pltpu.VMEM((2, 2, rows, 128), F32),
            pltpu.VMEM((slots, 128), F32),
            pltpu.VMEM((slots, 128), F32),
            pltpu.VMEM((slots, 128), F32),
            pltpu.VMEM((devices, 2, 128), F32),
            pltpu.VMEM((devices, 2, 128), F32),
            pltpu.VMEM((devices, 2, 128), F32),
            pltpu.VMEM((slots, 128), F32),
            pltpu.VMEM((256, slots * 128), BF16),
            pltpu.VMEM((128, slots * 128), BF16),
            pltpu.VMEM((2, 192, 128), F32),
            pltpu.VMEM((192, 256), BF16),
            pltpu.VMEM((devices, 3, 8, 128), BF16),
            pltpu.VMEM((devices, 3, 8, 128), BF16),
            pltpu.VMEM((128, G * 256), BF16),
            pltpu.VMEM((64, 128), F32),
            pltpu.VMEM((devices, 3, 4, 128), BF16),
            pltpu.VMEM((devices, 3, 4, 128), BF16),
            pltpu.VMEM((256, G * 256), BF16),
            pltpu.VMEM((128, 128), F32),
            pltpu.VMEM((256, 256), F32),
            dma((2, 4)),
            dma((2, 4)),
            dma(()),
            dma(()),
            dma(()),
            dma((devices // G,)),
            dma(()),
            dma((devices // G,)),
            dma((11,)),
            dma((3,)),
        ],
        compiler_params=pltpu.CompilerParams(
            collective_id=0, has_side_effects=True, vmem_limit_bytes=56 * 1024 * 1024
        ),
    )(
        atmos,
        diffusivity,
        sea_atm,
        flux_weight,
        block_owner.reshape(1, -1),
        entry_count.reshape(1, -1),
        source_col,
        dest_col,
        margin,
        ocean,
        sea_ocean.reshape(1, -1),
        couple,
        surface_weight,
    )
    return pl.pallas_call(
        hand_over,
        out_shape=shapes,
        in_specs=[far] * 3,
        out_specs=(far, far, far),
        scratch_shapes=[pltpu.VMEM(x.shape, F32) for x in shapes] + [dma((8,))],
    )(*results)


def solution(mesh):
    placed = (
        P(None, "grp", "tile"),
        P("grp", "tile"),
        P("grp", "tile"),
        P(),
        P(("grp", "tile"), None),
        P(("grp", "tile")),
        P(("grp", "tile"), None),
        P(("grp", "tile"), None),
        P(("grp", "tile"), None),
        P(None, ("grp", "tile")),
        P(("grp", "tile")),
        P(),
        P(),
    )
    return jax.shard_map(
        functools.partial(on_device, mesh.shape["grp"], mesh.shape["tile"]),
        mesh=mesh,
        in_specs=placed,
        out_specs=(P(None, "grp", "tile"), P(None, ("grp", "tile")), P(None, "grp", "tile")),
        check_vma=False,
    )
```

```python
import functools

import jax
import jax.numpy as jnp
from jax import lax
from jax.experimental import pallas as pl
from jax.experimental.pallas import tpu as pltpu
from jax.sharding import PartitionSpec as P

MESH = pl.DeviceIdType.MESH
F32, BF16, I32 = jnp.float32, jnp.bfloat16, jnp.int32
NT = (((1,), (1,)), ((), ()))
G = 8


def iota(shape, dim):
    return lax.broadcasted_iota(I32, shape, dim)


def rows_of(row, count):
    return jnp.broadcast_to(row, (count, row.shape[1]))


def remote(src, dst, send_sem, recv_sem, device):
    return pltpu.make_async_remote_copy(
        src_ref=src,
        dst_ref=dst,
        send_sem=send_sem,
        recv_sem=recv_sem,
        device_id=device,
        device_id_type=MESH,
    )


def kernel(
    grps,
    tiles,
    atmos_in,
    kappa_in,
    sea_atm_in,
    flux_w,
    owner,
    count,
    source_in,
    dest_in,
    margin_in,
    ocean_in,
    sea_oc,
    couple,
    surf_w,
    atmos_to,
    ocean_to,
    surf_to,
    atmos,
    kappa,
    sea_atm,
    source,
    dest,
    margin,
    ocean,
    atmos_out,
    ocean_out,
    atm_surf,
    mid,
    row_send,
    row_recv,
    col_send,
    col_recv,
    corner_recv,
    src_hi,
    src_lo,
    dst_all,
    dst_send,
    dst_recv,
    dst_hi,
    weight,
    hot_src,
    hot_dst,
    table32,
    table,
    fwd_send,
    fwd_recv,
    spread,
    surf32,
    back_send,
    back_recv,
    spread2,
    total,
    summed,
    halo_ss,
    halo_rs,
    dst_ss,
    dst_rs,
    fwd_ss,
    fwd_rs,
    back_ss,
    back_rs,
    in_sem,
    out_sem,
):
    devices = grps * tiles
    groups = devices // G
    width = G * 256
    g, t = lax.axis_index("grp"), lax.axis_index("tile")
    me = g * tiles + t

    z, y, core = t // 8, lax.rem(t // 2, 4), lax.rem(t, 2)

    def peer(i, j, back=False):
        s, c = j // 2, j % 2
        dz, dy = i // 4 + s, lax.rem(i, 4) + s
        if back:
            s, dz, dy = 4 - s, 8 - dz, 8 - dy
        row = lax.rem(z + dz, 4) * 8 + lax.rem(y + dy, 4) * 2 + lax.rem(core + c, 2)
        return (lax.rem(g + s, 4), row)

    def dest_copy(i, j):
        k = i * G + j
        return remote(dst_send.at[k], dst_recv.at[k], dst_ss, dst_rs, peer(i, j))

    def fwd_copy(i, j):
        k = i * G + j
        return remote(fwd_send.at[k], fwd_recv.at[k], fwd_ss, fwd_rs.at[i], peer(i, j))

    def back_copy(i, j):
        k = i * G + j
        return remote(back_send.at[k], back_recv.at[k], back_ss, back_rs.at[i], peer(i, j, True))

    def each_group(act):
        @pl.loop(1, groups)
        def _(i):
            act(i, 0)

        act(0, 1)

    def start_all(make):
        def act(i, first):
            for j in range(first, G):
                make(i, j).start()

        return act

    def settle(buffer, sem, start, size):
        part = buffer.at[pl.ds(start, size)]
        pltpu.make_async_copy(part, part, sem).wait()

    def settle_group(buffer, sems, i, first):
        settle(buffer, sems.at[i], i * G + first, G - first)

    loads = {}
    for n, (name, a, b) in enumerate(
        (
            ("atmos", atmos_in, atmos),
            ("kappa", kappa_in, kappa),
            ("source", source_in, source),
            ("dest", dest_in, dest),
            ("margin", margin_in, margin),
            ("sea", sea_atm_in, sea_atm),
            ("ocean", ocean_in, ocean),
        )
    ):
        loads[name] = pltpu.make_async_copy(a, b, in_sem.at[n])
        loads[name].start()

    barrier = pltpu.get_barrier_semaphore()

    def greet(i, first):
        for j in range(first, G):
            pl.semaphore_signal(barrier, inc=1, device_id=peer(i, j), device_id_type=MESH)

    each_group(greet)

    ids16 = (iota((16, 16, 128), 0) * 16 + iota((16, 16, 128), 1)).astype(F32).astype(BF16)
    ids8 = (iota((8, 16, 128), 0) * 16 + iota((8, 16, 128), 1)).astype(F32).astype(BF16)
    one, zero = jnp.ones((16, 128), BF16), jnp.zeros((16, 128), BF16)

    def place_blocks():
        blocks = owner.shape[1]
        own_row = owner[...]
        own_here = jnp.broadcast_to(own_row, (blocks, blocks)).astype(F32)
        own_col = jnp.transpose(own_here)
        cnt_col = jnp.transpose(jnp.broadcast_to(count[...], (blocks, blocks)).astype(F32))
        before = iota((blocks, blocks), 0) < iota((blocks, blocks), 1)
        same = jnp.where((own_here == own_col) & before, F32(1), F32(0))
        rank = jnp.sum(same, axis=0, keepdims=True).astype(I32)
        dx = ((own_row >> 5) - g) & 3
        dz = (((own_row >> 3) & 3) - z - dx) & 3
        dy = (((own_row >> 1) & 3) - y - dx) & 3
        dc = ((own_row & 1) - core) & 1
        slot = (((dz * 4 + dy) * 4 + dx) * 2 + dc) * 2 + rank
        place = jnp.where(
            iota((2 * devices, blocks), 0) == jnp.broadcast_to(slot, (2 * devices, blocks)), F32(1), F32(0)
        ).astype(BF16)

        def placed(values):
            return jnp.dot(place, values.astype(BF16), preferred_element_type=F32)

        src = source[...]
        src_hi[...] = placed((src >> 8).astype(F32))
        src_lo[...] = placed((src & 255).astype(F32))
        dst = dest[...]
        dst_all[...] = placed((dst >> 7).astype(F32)) * 128.0 + placed((dst & 127).astype(F32))

        @pl.loop(0, devices // 4)
        def _(i):
            four = dst_all[pl.ds(pl.multiple_of(i * 8, 8), 8), :]
            for j in range(4):
                dst_send[i * 4 + j] = four[2 * j : 2 * j + 2]

        dst_recv[0] = dst_send[0]
        lanes = iota((blocks, 128), 1).astype(F32)
        live = jnp.where(lanes < cnt_col[:, :1], margin[...], F32(0))
        first = live.astype(BF16).astype(F32)
        rest = live - first
        second = rest.astype(BF16).astype(F32)
        third = rest - second
        weight[...] = placed(first) + placed(second) + placed(third)

    rows, cols = atmos.shape[1], atmos.shape[2]
    chans = atmos.shape[0]
    row_id, col_id = iota((rows, cols), 0), iota((rows, cols), 1)
    lane = iota((rows, 128), 1)
    up_g, down_g = lax.rem(g + grps - 1, grps), lax.rem(g + 1, grps)
    left_t, right_t = lax.rem(t + tiles - 1, tiles), lax.rem(t + 1, tiles)
    edge_n, edge_s, edge_w, edge_e = g == 0, g == grps - 1, t == 0, t == tiles - 1
    loads["atmos"].wait()
    loads["kappa"].wait()
    diffusion = kappa[...]
    west = jnp.where(lane == 2 * chans, diffusion[:, 0:1], F32(0))
    east = jnp.where(lane == 2 * chans, diffusion[:, cols - 1 : cols], F32(0))
    for ch in range(chans):
        x = atmos[ch]
        far_ch = chans + ch
        row_send[0, ch : ch + 1, :] = x[0:1]
        row_send[0, far_ch : far_ch + 1, :] = x[1:2]
        row_send[1, ch : ch + 1, :] = x[rows - 1 : rows]
        row_send[1, far_ch : far_ch + 1, :] = x[rows - 2 : rows - 1]
        west = jnp.where(lane == ch, x[:, 0:1], west)
        west = jnp.where(lane == far_ch, x[:, 1:2], west)
        east = jnp.where(lane == ch, x[:, cols - 1 : cols], east)
        east = jnp.where(lane == far_ch, x[:, cols - 2 : cols - 1], east)
    row_send[0, 2 * chans : 2 * chans + 1, :] = diffusion[0:1]
    row_send[1, 2 * chans : 2 * chans + 1, :] = diffusion[rows - 1 : rows]
    col_send[0] = west
    col_send[1] = east
    top, bottom = pl.ds(0, 8), pl.ds(rows - 8, 8)
    plan = (
        (row_send.at[0], row_recv.at[1], (up_g, t)),
        (row_send.at[1], row_recv.at[0], (down_g, t)),
        (col_send.at[0], col_recv.at[1], (g, left_t)),
        (col_send.at[1], col_recv.at[0], (g, right_t)),
        (col_send.at[0, top], corner_recv.at[3], (up_g, left_t)),
        (col_send.at[1, top], corner_recv.at[2], (up_g, right_t)),
        (col_send.at[0, bottom], corner_recv.at[1], (down_g, left_t)),
        (col_send.at[1, bottom], corner_recv.at[0], (down_g, right_t)),
    )
    copies = [
        remote(src, dst, halo_ss.at[n], halo_rs.at[n], device)
        for n, (src, dst, device) in enumerate(plan)
    ]
    pl.semaphore_wait(barrier, devices - 1)
    for copy in copies:
        copy.start()
    for name in ("source", "dest", "margin", "sea", "ocean"):
        loads[name].wait()
    place_blocks()
    each_group(start_all(dest_copy))
    for copy in copies:
        copy.wait()

    nw = jnp.where(edge_n | edge_w, F32(0), corner_recv[0, 7:8, :])
    ne = jnp.where(edge_n | edge_e, F32(0), corner_recv[1, 7:8, :])
    sw = jnp.where(edge_s | edge_w, F32(0), corner_recv[2, 0:1, :])
    se = jnp.where(edge_s | edge_e, F32(0), corner_recv[3, 0:1, :])

    def upright(row):
        spot = jnp.where(lane == iota((rows, 128), 0), jnp.broadcast_to(row, (rows, 128)), F32(0))
        return jnp.sum(spot, axis=1, keepdims=True)

    def line(here, below, above, at_left, at_right, rate):
        left = jnp.where(col_id == 0, upright(at_left), pltpu.roll(here, 1, 1))
        right = jnp.where(col_id == cols - 1, upright(at_right), pltpu.roll(here, cols - 1, 1))
        return here + rate * (below + above + right + left - 4.0 * here)

    row_lane = iota((rows, 128), 0)

    def column(here, right, left, at_top, at_bottom, rate):
        above = jnp.where(row_lane == 0, at_top, pltpu.roll(here, 1, 0))
        below = jnp.where(row_lane == rows - 1, at_bottom, pltpu.roll(here, rows - 1, 0))
        return here + rate * (below + above + right + left - 4.0 * here)

    north = jnp.where(edge_n, F32(0), row_recv[0, 0:chans, :])
    north2 = jnp.where(edge_n, F32(0), row_recv[0, chans : 2 * chans, :])
    south = jnp.where(edge_s, F32(0), row_recv[1, 0:chans, :])
    south2 = jnp.where(edge_s, F32(0), row_recv[1, chans : 2 * chans, :])
    west = jnp.where(edge_w, F32(0), col_recv[0])
    east = jnp.where(edge_e, F32(0), col_recv[1])
    rim = [
        (north, south, west, east),
        (
            jnp.where(
                edge_n,
                F32(0),
                line(
                    north,
                    row_send[0, 0:chans, :],
                    north2,
                    nw,
                    ne,
                    row_recv[0, 2 * chans : 2 * chans + 1, :],
                ),
            ),
            jnp.where(
                edge_s,
                F32(0),
                line(
                    south,
                    south2,
                    row_send[1, 0:chans, :],
                    sw,
                    se,
                    row_recv[1, 2 * chans : 2 * chans + 1, :],
                ),
            ),
            jnp.where(
                edge_w,
                F32(0),
                column(
                    west,
                    col_send[0],
                    pltpu.roll(west, 128 - chans, 1),
                    nw,
                    sw,
                    col_recv[0, :, 2 * chans : 2 * chans + 1],
                ),
            ),
            jnp.where(
                edge_e,
                F32(0),
                column(
                    east,
                    pltpu.roll(east, 128 - chans, 1),
                    col_send[1],
                    ne,
                    se,
                    col_recv[1, :, 2 * chans : 2 * chans + 1],
                ),
            ),
        ),
    ]
    for step in range(2):
        state, after = (atmos, mid) if step == 0 else (mid, atmos_out)
        north, south, west, east = rim[step]
        for ch in range(chans):
            x = state[ch]
            up = jnp.where(row_id == 0, north[ch : ch + 1], pltpu.roll(x, 1, 0))
            down = jnp.where(row_id == rows - 1, south[ch : ch + 1], pltpu.roll(x, rows - 1, 0))
            left = jnp.where(col_id == 0, west[:, ch : ch + 1], pltpu.roll(x, 1, 1))
            right = jnp.where(col_id == cols - 1, east[:, ch : ch + 1], pltpu.roll(x, cols - 1, 1))
            after[ch] = x + diffusion * (down + up + right + left - 4.0 * x)

    stores = [pltpu.make_async_copy(atmos_out, atmos_to, out_sem.at[0])]
    stores[0].start()

    sea = sea_atm[...] > 0
    for f in range(12):
        mixed = flux_w[f, 0] * atmos_out[0]
        for ch in range(1, chans):
            mixed = mixed + flux_w[f, ch] * atmos_out[ch]
        flux = jnp.where(sea, jnp.tanh(mixed), F32(0))
        for half in range(2):
            part = flux[:, half * 128 : half * 128 + 128]
            if f < 8:
                table32[half, pl.ds(f, 16, stride=8), :] = part
            else:
                table32[half, pl.ds(128 + f - 8, 16, stride=4), :] = part
    for half in range(2):
        full = table32[half]
        table[:, half * 128 : half * 128 + 128] = full.astype(BF16)

    sub = iota((8, 128), 0)
    odd = jnp.where(sub >= 4, F32(1), F32(0))

    def give(i, first):
        here = pl.ds(pl.multiple_of(i * 2 * G, 2 * G), 2 * G)
        low = src_lo[here, :]
        hi, w = src_hi[here, :], weight[here, :]
        for j in range(G):
            hots = []
            for part in range(2):
                lo = rows_of(low[2 * j + part : 2 * j + part + 1], 16).astype(BF16)
                hots.append(jnp.where(ids16 == lo[None], one[None], zero[None]).reshape(256, 128))
            hot = jnp.concatenate(hots, axis=1)
            hot_src[:, pl.ds(pl.multiple_of(i * width + j * 256, 256), 256)] = hot
            found = jnp.dot(table[...], hot, preferred_element_type=F32)
            ends = []
            for part in range(2):
                mine = found[:, part * 128 : part * 128 + 128]
                h = rows_of(hi[2 * j + part : 2 * j + part + 1], 8)
                wide = mine[0:8]
                for v in range(1, 16):
                    wide = jnp.where(h == v, mine[v * 8 : v * 8 + 8], wide)
                h = h - odd
                thin = jnp.zeros((8, 128), F32)
                for v in range(8):
                    thin = jnp.where(h == 2 * v, mine[128 + v * 8 : 136 + v * 8], thin)
                scale = rows_of(w[2 * j + part : 2 * j + part + 1], 8)
                fwd_send[i * G + j, part] = (wide * scale).astype(BF16)
                ends.append((thin + pltpu.roll(thin, 4, 0)) * scale)
            fwd_send[i * G + j, 2] = jnp.where(sub < 4, ends[0], ends[1]).astype(BF16)
        start_all(fwd_copy)(i, first)

    each_group(give)

    fwd_recv[0] = fwd_send[0]

    settle(dst_recv, dst_rs, 1, devices - 1)

    @pl.loop(0, groups)
    def _(i):
        for j in range(G):
            where = dst_recv[i * G + j]
            high = jnp.floor(where * (1 / 128))
            dst_hi[i * G + j] = high
            low = where - high * 128.0
            for part in range(2):
                lo = rows_of(low[part : part + 1], 16).astype(BF16)
                hot = jnp.where(ids8 == lo[None], one[None], zero[None])
                hot_dst[:, pl.ds(pl.multiple_of(i * width + j * 256 + part * 128, 128), 128)] = hot.reshape(
                    128, 128
                )

    total[...] = jnp.zeros_like(total)

    def collect(i, first):
        settle_group(fwd_recv, fwd_rs, i, first)
        for j in range(G):
            high = dst_hi[i * G + j]
            ends = fwd_recv[i * G + j, 2].astype(F32)
            for part in range(2):
                tile = jnp.concatenate(
                    [fwd_recv[i * G + j, part].astype(F32), pltpu.roll(ends, 4, 0) if part else ends],
                    axis=0,
                ).astype(BF16)
                hi = rows_of(high[part : part + 1], 16).astype(BF16)
                at = slice(j * 256 + part * 128, j * 256 + part * 128 + 128)
                for v in range(8):
                    spread[v * 16 : v * 16 + 16, at] = jnp.where(hi == v, tile, zero)
        total[...] += lax.dot_general(
            spread[...],
            hot_dst[:, pl.ds(pl.multiple_of(i * width, width), width)],
            NT,
            preferred_element_type=F32,
        )

    each_group(collect)

    surf32[...] = jnp.zeros_like(surf32)
    for h in range(8):
        here = slice(h * 128, h * 128 + 128)
        flux = total[h * 16 : h * 16 + 16, :]
        added = couple[:, 0:1] * flux[0:1]
        for f in range(1, 12):
            added = added + couple[:, f : f + 1] * flux[f : f + 1]
        new = ocean[:, here] + jnp.where(sea_oc[:, here] > 0, added, F32(0))
        ocean_out[:, here] = new
        field = surf_w[:, 0:1] * new[0:1]
        for o in range(1, 8):
            field = field + surf_w[:, o : o + 1] * new[o : o + 1]
        surf32[h * 8 : h * 8 + 6, :] = jnp.tanh(field)
    surface = surf32[...].astype(BF16)
    stores.append(pltpu.make_async_copy(ocean_out, ocean_to, out_sem.at[1]))
    stores[1].start()

    def answer(i, first):
        for j in range(G):
            k = i * G + j
            found = jnp.dot(
                surface,
                hot_dst[:, pl.ds(pl.multiple_of(i * width + j * 256, 256), 256)],
                preferred_element_type=F32,
            )
            high = dst_hi[k]
            both = []
            for part in range(2):
                mine = found[:, part * 128 : part * 128 + 128]
                h = rows_of(high[part : part + 1], 8)
                got = mine[0:8]
                for v in range(1, 8):
                    got = jnp.where(h == v, mine[v * 8 : v * 8 + 8], got)
                back_send[k, part] = got[0:4].astype(BF16)
                both.append(got)
            ends = jnp.where(sub < 2, pltpu.roll(both[0], 4, 0), pltpu.roll(both[1], 6, 0))
            back_send[k, 2] = ends[0:4].astype(BF16)
        start_all(back_copy)(i, first)

    each_group(answer)

    back_recv[0] = back_send[0]

    summed[...] = jnp.zeros_like(summed)

    def gather_up(i, first):
        settle_group(back_recv, back_rs, i, first)
        here = pl.ds(pl.multiple_of(i * 2 * G, 2 * G), 2 * G)
        hi, w = src_hi[here, :], weight[here, :]
        for j in range(G):
            ends = back_recv[i * G + j, 2].astype(F32)
            for part in range(2):
                most = back_recv[i * G + j, part].astype(F32)
                last = [ends[2:4], ends[0:2]] if part else [ends]
                value = jnp.concatenate([most] + last, axis=0)
                value = value * rows_of(w[2 * j + part : 2 * j + part + 1], 8)
                top = value.astype(BF16).astype(F32)
                pair = jnp.concatenate([top, value - top], axis=0).astype(BF16)
                h = rows_of(hi[2 * j + part : 2 * j + part + 1], 16).astype(BF16)
                at = slice(j * 256 + part * 128, j * 256 + part * 128 + 128)
                for v in range(16):
                    spread2[v * 16 : v * 16 + 16, at] = jnp.where(h == v, pair, zero)
        added = lax.dot_general(
            spread2[...],
            hot_src[:, pl.ds(pl.multiple_of(i * width, width), width)],
            NT,
            preferred_element_type=F32,
        )
        summed[...] += added

    each_group(gather_up)

    for half in range(2):
        here = slice(half * 128, half * 128 + 128)
        for h in range(16):
            table32[half, h * 8 : h * 8 + 8, :] = (
                summed[h * 16 : h * 16 + 8, here] + summed[h * 16 + 8 : h * 16 + 16, here]
            )
        for s in range(6):
            atm_surf[s, :, here] = jnp.where(
                sea[:, here], table32[half, pl.ds(s, 16, stride=8), :], F32(0)
            )

    stores.append(pltpu.make_async_copy(atm_surf, surf_to, out_sem.at[2]))
    stores[2].start()
    for copy in stores:
        copy.wait()

    settle(dst_send, dst_ss, 1, devices - 1)
    settle(fwd_send, fwd_ss, 1, devices - 1)
    settle(back_send, back_ss, 1, devices - 1)


def hand_over(a, b, c, a_to, b_to, c_to, a_here, b_here, c_here, sem):
    here = (a_here.at[pl.ds(0, 8)], a_here.at[pl.ds(8, 8)], b_here, c_here)
    into = (a.at[pl.ds(0, 8)], a.at[pl.ds(8, 8)], b, c)
    out = (a_to.at[pl.ds(0, 8)], a_to.at[pl.ds(8, 8)], b_to, c_to)
    loads = [pltpu.make_async_copy(into[n], here[n], sem.at[n]) for n in range(4)]
    stores = [pltpu.make_async_copy(here[n], out[n], sem.at[4 + n]) for n in range(4)]
    for copy in loads:
        copy.start()
    for n in range(4):
        loads[n].wait()
        stores[n].start()
    for copy in stores:
        copy.wait()


def on_device(grps, tiles, *args):
    (
        atmos,
        diffusivity,
        sea_atm,
        flux_weight,
        block_owner,
        entry_count,
        source_col,
        dest_col,
        margin,
        ocean,
        sea_ocean,
        couple,
        surface_weight,
    ) = args
    devices = grps * tiles
    slots = 2 * devices
    vmem = pl.BlockSpec(memory_space=pltpu.VMEM)
    smem = pl.BlockSpec(memory_space=pltpu.SMEM)
    far = pl.BlockSpec(memory_space=pl.ANY)
    chans, rows, cols = atmos.shape
    dma = pltpu.SemaphoreType.DMA
    shapes = (
        jax.ShapeDtypeStruct(atmos.shape, F32),
        jax.ShapeDtypeStruct(ocean.shape, F32),
        jax.ShapeDtypeStruct((6, rows, cols), F32),
    )
    results = pl.pallas_call(
        functools.partial(kernel, grps, tiles),
        out_shape=shapes,
        in_specs=[far, far, far, smem, vmem, vmem, far, far, far, far, vmem, vmem, vmem],
        out_specs=(far, far, far),
        scratch_shapes=[
            pltpu.VMEM((chans, rows, cols), F32),
            pltpu.VMEM((rows, cols), F32),
            pltpu.VMEM((rows, cols), I32),
            pltpu.VMEM(source_col.shape, I32),
            pltpu.VMEM(source_col.shape, I32),
            pltpu.VMEM(source_col.shape, F32),
            pltpu.VMEM(ocean.shape, F32),
            pltpu.VMEM((chans, rows, cols), F32),
            pltpu.VMEM(ocean.shape, F32),
            pltpu.VMEM((6, rows, cols), F32),
            pltpu.VMEM((chans, rows, cols), F32),
            pltpu.VMEM((2, 2 * chans + 1, cols), F32),
            pltpu.VMEM((2, 2 * chans + 1, cols), F32),
            pltpu.VMEM((2, rows, 128), F32),
            pltpu.VMEM((2, rows, 128), F32),
            pltpu.VMEM((4, 8, 128), F32),
            pltpu.VMEM((slots, 128), F32),
            pltpu.VMEM((slots, 128), F32),
            pltpu.VMEM((slots, 128), F32),
            pltpu.VMEM((devices, 2, 128), F32),
            pltpu.VMEM((devices, 2, 128), F32),
            pltpu.VMEM((devices, 2, 128), F32),
            pltpu.VMEM((slots, 128), F32),
            pltpu.VMEM((256, slots * 128), BF16),
            pltpu.VMEM((128, slots * 128), BF16),
            pltpu.VMEM((2, 192, 128), F32),
            pltpu.VMEM((192, 256), BF16),
            pltpu.VMEM((devices, 3, 8, 128), BF16),
            pltpu.VMEM((devices, 3, 8, 128), BF16),
            pltpu.VMEM((128, G * 256), BF16),
            pltpu.VMEM((64, 128), F32),
            pltpu.VMEM((devices, 3, 4, 128), BF16),
            pltpu.VMEM((devices, 3, 4, 128), BF16),
            pltpu.VMEM((256, G * 256), BF16),
            pltpu.VMEM((128, 128), F32),
            pltpu.VMEM((256, 256), F32),
            dma((8,)),
            dma((8,)),
            dma(()),
            dma(()),
            dma(()),
            dma((devices // G,)),
            dma(()),
            dma((devices // G,)),
            dma((11,)),
            dma((3,)),
        ],
        compiler_params=pltpu.CompilerParams(
            collective_id=0, has_side_effects=True, vmem_limit_bytes=56 * 1024 * 1024
        ),
    )(
        atmos,
        diffusivity,
        sea_atm,
        flux_weight,
        block_owner.reshape(1, -1),
        entry_count.reshape(1, -1),
        source_col,
        dest_col,
        margin,
        ocean,
        sea_ocean.reshape(1, -1),
        couple,
        surface_weight,
    )
    return pl.pallas_call(
        hand_over,
        out_shape=shapes,
        in_specs=[far] * 3,
        out_specs=(far, far, far),
        scratch_shapes=[pltpu.VMEM(x.shape, F32) for x in shapes] + [dma((8,))],
    )(*results)


def solution(mesh):
    placed = (
        P(None, "grp", "tile"),
        P("grp", "tile"),
        P("grp", "tile"),
        P(),
        P(("grp", "tile"), None),
        P(("grp", "tile")),
        P(("grp", "tile"), None),
        P(("grp", "tile"), None),
        P(("grp", "tile"), None),
        P(None, ("grp", "tile")),
        P(("grp", "tile")),
        P(),
        P(),
    )
    return jax.shard_map(
        functools.partial(on_device, mesh.shape["grp"], mesh.shape["tile"]),
        mesh=mesh,
        in_specs=placed,
        out_specs=(P(None, "grp", "tile"), P(None, ("grp", "tile")), P(None, "grp", "tile")),
        check_vma=False,
    )
```

```python
import functools

import jax
import jax.numpy as jnp
from jax import lax
from jax.experimental import pallas as pl
from jax.experimental.pallas import tpu as pltpu
from jax.sharding import PartitionSpec as P

MESH = pl.DeviceIdType.MESH
F32, BF16, I32 = jnp.float32, jnp.bfloat16, jnp.int32
NT = (((1,), (1,)), ((), ()))
G = 8


def iota(shape, dim):
    return lax.broadcasted_iota(I32, shape, dim)


def rows_of(row, count):
    return jnp.broadcast_to(row, (count, row.shape[1]))


def remote(src, dst, send_sem, recv_sem, device):
    return pltpu.make_async_remote_copy(
        src_ref=src,
        dst_ref=dst,
        send_sem=send_sem,
        recv_sem=recv_sem,
        device_id=device,
        device_id_type=MESH,
    )


def kernel(
    grps,
    tiles,
    atmos_in,
    kappa_in,
    sea_atm_in,
    flux_w,
    owner,
    count,
    source_in,
    dest_in,
    margin_in,
    ocean_in,
    sea_oc,
    couple,
    surf_w,
    atmos_to,
    ocean_to,
    surf_to,
    atmos,
    kappa,
    sea_atm,
    source,
    dest,
    margin,
    ocean,
    atmos_out,
    ocean_out,
    atm_surf,
    mid,
    row_send,
    row_recv,
    col_send,
    col_recv,
    corner_recv,
    src_hi,
    src_lo,
    dst_all,
    dst_send,
    dst_recv,
    dst_hi,
    weight,
    hot_src,
    hot_dst,
    table32,
    table,
    fwd_send,
    fwd_recv,
    spread,
    surf32,
    back_send,
    back_recv,
    spread2,
    spread3,
    total,
    summed,
    halo_ss,
    halo_rs,
    dst_ss,
    dst_rs,
    fwd_ss,
    fwd_rs,
    back_ss,
    back_rs,
    in_sem,
    out_sem,
):
    devices = grps * tiles
    groups = devices // G
    width = G * 256
    g, t = lax.axis_index("grp"), lax.axis_index("tile")
    me = g * tiles + t

    z, y, core = t // 8, lax.rem(t // 2, 4), lax.rem(t, 2)

    def peer(i, j, back=False):
        s, c = j // 2, j % 2
        dz, dy = i // 4 + s, lax.rem(i, 4) + s
        if back:
            s, dz, dy = 4 - s, 8 - dz, 8 - dy
        row = lax.rem(z + dz, 4) * 8 + lax.rem(y + dy, 4) * 2 + lax.rem(core + c, 2)
        return (lax.rem(g + s, 4), row)

    def dest_copy(i, j):
        k = i * G + j
        return remote(dst_send.at[k], dst_recv.at[k], dst_ss, dst_rs, peer(i, j))

    def fwd_copy(i, j):
        k = i * G + j
        return remote(fwd_send.at[k], fwd_recv.at[k], fwd_ss, fwd_rs.at[i], peer(i, j))

    def back_copy(i, j):
        k = i * G + j
        return remote(back_send.at[k], back_recv.at[k], back_ss, back_rs.at[i], peer(i, j, True))

    def each_group(act):
        @pl.loop(1, groups)
        def _(i):
            act(i, 0)

        act(0, 1)

    def start_all(make):
        def act(i, first):
            for j in range(first, G):
                make(i, j).start()

        return act

    def settle(buffer, sem, start, size):
        part = buffer.at[pl.ds(start, size)]
        pltpu.make_async_copy(part, part, sem).wait()

    def settle_group(buffer, sems, i, first):
        settle(buffer, sems.at[i], i * G + first, G - first)

    loads = {}
    for n, (name, a, b) in enumerate(
        (
            ("atmos", atmos_in, atmos),
            ("kappa", kappa_in, kappa),
            ("source", source_in, source),
            ("dest", dest_in, dest),
            ("margin", margin_in, margin),
            ("sea", sea_atm_in, sea_atm),
            ("ocean", ocean_in, ocean),
        )
    ):
        loads[name] = pltpu.make_async_copy(a, b, in_sem.at[n])
        loads[name].start()

    barrier = pltpu.get_barrier_semaphore()

    def greet(i, first):
        for j in range(first, G):
            pl.semaphore_signal(barrier, inc=1, device_id=peer(i, j), device_id_type=MESH)

    each_group(greet)

    ids16 = (iota((16, 16, 128), 0) * 16 + iota((16, 16, 128), 1)).astype(F32).astype(BF16)
    ids8 = (iota((8, 16, 128), 0) * 16 + iota((8, 16, 128), 1)).astype(F32).astype(BF16)
    one, zero = jnp.ones((16, 128), BF16), jnp.zeros((16, 128), BF16)

    def place_blocks():
        blocks = owner.shape[1]
        own_row = owner[...]
        own_here = jnp.broadcast_to(own_row, (blocks, blocks)).astype(F32)
        own_col = jnp.transpose(own_here)
        cnt_col = jnp.transpose(jnp.broadcast_to(count[...], (blocks, blocks)).astype(F32))
        before = iota((blocks, blocks), 0) < iota((blocks, blocks), 1)
        same = jnp.where((own_here == own_col) & before, F32(1), F32(0))
        rank = jnp.sum(same, axis=0, keepdims=True).astype(I32)
        dx = ((own_row >> 5) - g) & 3
        dz = (((own_row >> 3) & 3) - z - dx) & 3
        dy = (((own_row >> 1) & 3) - y - dx) & 3
        dc = ((own_row & 1) - core) & 1
        slot = (((dz * 4 + dy) * 4 + dx) * 2 + dc) * 2 + rank
        place = jnp.where(
            iota((2 * devices, blocks), 0) == jnp.broadcast_to(slot, (2 * devices, blocks)), F32(1), F32(0)
        ).astype(BF16)

        def placed(values):
            return jnp.dot(place, values.astype(BF16), preferred_element_type=F32)

        src = source[...]
        src_hi[...] = placed((src >> 8).astype(F32))
        src_lo[...] = placed((src & 255).astype(F32))
        dst = dest[...]
        dst_all[...] = placed((dst >> 7).astype(F32)) * 128.0 + placed((dst & 127).astype(F32))

        @pl.loop(0, devices // 4)
        def _(i):
            four = dst_all[pl.ds(pl.multiple_of(i * 8, 8), 8), :]
            for j in range(4):
                dst_send[i * 4 + j] = four[2 * j : 2 * j + 2]

        dst_recv[0] = dst_send[0]
        lanes = iota((blocks, 128), 1).astype(F32)
        live = jnp.where(lanes < cnt_col[:, :1], margin[...], F32(0))
        first = live.astype(BF16).astype(F32)
        rest = live - first
        second = rest.astype(BF16).astype(F32)
        third = rest - second
        weight[...] = placed(first) + placed(second) + placed(third)

    rows, cols = atmos.shape[1], atmos.shape[2]
    chans = atmos.shape[0]
    row_id, col_id = iota((rows, cols), 0), iota((rows, cols), 1)
    lane = iota((rows, 128), 1)
    up_g, down_g = lax.rem(g + grps - 1, grps), lax.rem(g + 1, grps)
    left_t, right_t = lax.rem(t + tiles - 1, tiles), lax.rem(t + 1, tiles)
    edge_n, edge_s, edge_w, edge_e = g == 0, g == grps - 1, t == 0, t == tiles - 1
    loads["atmos"].wait()
    loads["kappa"].wait()
    diffusion = kappa[...]
    west = jnp.where(lane == 2 * chans, diffusion[:, 0:1], F32(0))
    east = jnp.where(lane == 2 * chans, diffusion[:, cols - 1 : cols], F32(0))
    for ch in range(chans):
        x = atmos[ch]
        far_ch = chans + ch
        row_send[0, ch : ch + 1, :] = x[0:1]
        row_send[0, far_ch : far_ch + 1, :] = x[1:2]
        row_send[1, ch : ch + 1, :] = x[rows - 1 : rows]
        row_send[1, far_ch : far_ch + 1, :] = x[rows - 2 : rows - 1]
        west = jnp.where(lane == ch, x[:, 0:1], west)
        west = jnp.where(lane == far_ch, x[:, 1:2], west)
        east = jnp.where(lane == ch, x[:, cols - 1 : cols], east)
        east = jnp.where(lane == far_ch, x[:, cols - 2 : cols - 1], east)
    row_send[0, 2 * chans : 2 * chans + 1, :] = diffusion[0:1]
    row_send[1, 2 * chans : 2 * chans + 1, :] = diffusion[rows - 1 : rows]
    col_send[0] = west
    col_send[1] = east
    top, bottom = pl.ds(0, 8), pl.ds(rows - 8, 8)
    plan = (
        (row_send.at[0], row_recv.at[1], (up_g, t)),
        (row_send.at[1], row_recv.at[0], (down_g, t)),
        (col_send.at[0], col_recv.at[1], (g, left_t)),
        (col_send.at[1], col_recv.at[0], (g, right_t)),
        (col_send.at[0, top], corner_recv.at[3], (up_g, left_t)),
        (col_send.at[1, top], corner_recv.at[2], (up_g, right_t)),
        (col_send.at[0, bottom], corner_recv.at[1], (down_g, left_t)),
        (col_send.at[1, bottom], corner_recv.at[0], (down_g, right_t)),
    )
    copies = [
        remote(src, dst, halo_ss.at[n], halo_rs.at[n], device)
        for n, (src, dst, device) in enumerate(plan)
    ]
    pl.semaphore_wait(barrier, devices - 1)
    for copy in copies:
        copy.start()
    for name in ("source", "dest", "margin", "sea", "ocean"):
        loads[name].wait()
    place_blocks()
    each_group(start_all(dest_copy))
    for copy in copies:
        copy.wait()

    nw = jnp.where(edge_n | edge_w, F32(0), corner_recv[0, 7:8, :])
    ne = jnp.where(edge_n | edge_e, F32(0), corner_recv[1, 7:8, :])
    sw = jnp.where(edge_s | edge_w, F32(0), corner_recv[2, 0:1, :])
    se = jnp.where(edge_s | edge_e, F32(0), corner_recv[3, 0:1, :])

    def upright(row):
        spot = jnp.where(lane == iota((rows, 128), 0), jnp.broadcast_to(row, (rows, 128)), F32(0))
        return jnp.sum(spot, axis=1, keepdims=True)

    def line(here, below, above, at_left, at_right, rate):
        left = jnp.where(col_id == 0, upright(at_left), pltpu.roll(here, 1, 1))
        right = jnp.where(col_id == cols - 1, upright(at_right), pltpu.roll(here, cols - 1, 1))
        return here + rate * (below + above + right + left - 4.0 * here)

    row_lane = iota((rows, 128), 0)

    def column(here, right, left, at_top, at_bottom, rate):
        above = jnp.where(row_lane == 0, at_top, pltpu.roll(here, 1, 0))
        below = jnp.where(row_lane == rows - 1, at_bottom, pltpu.roll(here, rows - 1, 0))
        return here + rate * (below + above + right + left - 4.0 * here)

    north = jnp.where(edge_n, F32(0), row_recv[0, 0:chans, :])
    north2 = jnp.where(edge_n, F32(0), row_recv[0, chans : 2 * chans, :])
    south = jnp.where(edge_s, F32(0), row_recv[1, 0:chans, :])
    south2 = jnp.where(edge_s, F32(0), row_recv[1, chans : 2 * chans, :])
    west = jnp.where(edge_w, F32(0), col_recv[0])
    east = jnp.where(edge_e, F32(0), col_recv[1])
    rim = [
        (north, south, west, east),
        (
            jnp.where(
                edge_n,
                F32(0),
                line(
                    north,
                    row_send[0, 0:chans, :],
                    north2,
                    nw,
                    ne,
                    row_recv[0, 2 * chans : 2 * chans + 1, :],
                ),
            ),
            jnp.where(
                edge_s,
                F32(0),
                line(
                    south,
                    south2,
                    row_send[1, 0:chans, :],
                    sw,
                    se,
                    row_recv[1, 2 * chans : 2 * chans + 1, :],
                ),
            ),
            jnp.where(
                edge_w,
                F32(0),
                column(
                    west,
                    col_send[0],
                    pltpu.roll(west, 128 - chans, 1),
                    nw,
                    sw,
                    col_recv[0, :, 2 * chans : 2 * chans + 1],
                ),
            ),
            jnp.where(
                edge_e,
                F32(0),
                column(
                    east,
                    pltpu.roll(east, 128 - chans, 1),
                    col_send[1],
                    ne,
                    se,
                    col_recv[1, :, 2 * chans : 2 * chans + 1],
                ),
            ),
        ),
    ]
    for step in range(2):
        state, after = (atmos, mid) if step == 0 else (mid, atmos_out)
        north, south, west, east = rim[step]
        for ch in range(chans):
            x = state[ch]
            up = jnp.where(row_id == 0, north[ch : ch + 1], pltpu.roll(x, 1, 0))
            down = jnp.where(row_id == rows - 1, south[ch : ch + 1], pltpu.roll(x, rows - 1, 0))
            left = jnp.where(col_id == 0, west[:, ch : ch + 1], pltpu.roll(x, 1, 1))
            right = jnp.where(col_id == cols - 1, east[:, ch : ch + 1], pltpu.roll(x, cols - 1, 1))
            after[ch] = x + diffusion * (down + up + right + left - 4.0 * x)

    stores = [pltpu.make_async_copy(atmos_out, atmos_to, out_sem.at[0])]
    stores[0].start()

    sea = sea_atm[...] > 0
    for f in range(12):
        mixed = flux_w[f, 0] * atmos_out[0]
        for ch in range(1, chans):
            mixed = mixed + flux_w[f, ch] * atmos_out[ch]
        flux = jnp.where(sea, jnp.tanh(mixed), F32(0))
        for half in range(2):
            part = flux[:, half * 128 : half * 128 + 128]
            if f < 8:
                table32[half, pl.ds(f, 16, stride=8), :] = part
            else:
                table32[half, pl.ds(128 + f - 8, 16, stride=4), :] = part
    for half in range(2):
        full = table32[half]
        table[:, half * 128 : half * 128 + 128] = full.astype(BF16)

    sub = iota((8, 128), 0)
    odd = jnp.where(sub >= 4, F32(1), F32(0))

    def give(i, first):
        here = pl.ds(pl.multiple_of(i * 2 * G, 2 * G), 2 * G)
        low = src_lo[here, :]
        hi, w = src_hi[here, :], weight[here, :]
        for j in range(G):
            hots = []
            for part in range(2):
                lo = rows_of(low[2 * j + part : 2 * j + part + 1], 16).astype(BF16)
                hots.append(jnp.where(ids16 == lo[None], one[None], zero[None]).reshape(256, 128))
            hot = jnp.concatenate(hots, axis=1)
            hot_src[:, pl.ds(pl.multiple_of(i * width + j * 256, 256), 256)] = hot
            found = jnp.dot(table[...], hot, preferred_element_type=F32)
            ends = []
            for part in range(2):
                mine = found[:, part * 128 : part * 128 + 128]
                h = rows_of(hi[2 * j + part : 2 * j + part + 1], 8)
                wide = mine[0:8]
                for v in range(1, 16):
                    wide = jnp.where(h == v, mine[v * 8 : v * 8 + 8], wide)
                h = h - odd
                thin = jnp.zeros((8, 128), F32)
                for v in range(8):
                    thin = jnp.where(h == 2 * v, mine[128 + v * 8 : 136 + v * 8], thin)
                scale = rows_of(w[2 * j + part : 2 * j + part + 1], 8)
                fwd_send[i * G + j, part] = (wide * scale).astype(BF16)
                ends.append((thin + pltpu.roll(thin, 4, 0)) * scale)
            fwd_send[i * G + j, 2] = jnp.where(sub < 4, ends[0], ends[1]).astype(BF16)
        start_all(fwd_copy)(i, first)

    each_group(give)

    fwd_recv[0] = fwd_send[0]

    settle(dst_recv, dst_rs, 1, devices - 1)

    @pl.loop(0, groups)
    def _(i):
        for j in range(G):
            where = dst_recv[i * G + j]
            high = jnp.floor(where * (1 / 128))
            dst_hi[i * G + j] = high
            low = where - high * 128.0
            for part in range(2):
                lo = rows_of(low[part : part + 1], 16).astype(BF16)
                hot = jnp.where(ids8 == lo[None], one[None], zero[None])
                hot_dst[:, pl.ds(pl.multiple_of(i * width + j * 256 + part * 128, 128), 128)] = hot.reshape(
                    128, 128
                )

    total[...] = jnp.zeros_like(total)

    def collect(i, first):
        settle_group(fwd_recv, fwd_rs, i, first)
        for j in range(G):
            high = dst_hi[i * G + j]
            ends = fwd_recv[i * G + j, 2].astype(F32)
            for part in range(2):
                tile = jnp.concatenate(
                    [fwd_recv[i * G + j, part].astype(F32), pltpu.roll(ends, 4, 0) if part else ends],
                    axis=0,
                ).astype(BF16)
                hi = rows_of(high[part : part + 1], 16).astype(BF16)
                at = slice(j * 256 + part * 128, j * 256 + part * 128 + 128)
                for v in range(8):
                    spread[v * 16 : v * 16 + 16, at] = jnp.where(hi == v, tile, zero)
        total[...] += lax.dot_general(
            spread[...],
            hot_dst[:, pl.ds(pl.multiple_of(i * width, width), width)],
            NT,
            preferred_element_type=F32,
        )

    each_group(collect)

    surf32[...] = jnp.zeros_like(surf32)
    for h in range(8):
        here = slice(h * 128, h * 128 + 128)
        flux = total[h * 16 : h * 16 + 16, :]
        added = couple[:, 0:1] * flux[0:1]
        for f in range(1, 12):
            added = added + couple[:, f : f + 1] * flux[f : f + 1]
        new = ocean[:, here] + jnp.where(sea_oc[:, here] > 0, added, F32(0))
        ocean_out[:, here] = new
        field = surf_w[:, 0:1] * new[0:1]
        for o in range(1, 8):
            field = field + surf_w[:, o : o + 1] * new[o : o + 1]
        surf32[h * 8 : h * 8 + 6, :] = jnp.tanh(field)
    surface = surf32[...].astype(BF16)
    stores.append(pltpu.make_async_copy(ocean_out, ocean_to, out_sem.at[1]))
    stores[1].start()

    def answer(i, first):
        for j in range(G):
            k = i * G + j
            found = jnp.dot(
                surface,
                hot_dst[:, pl.ds(pl.multiple_of(i * width + j * 256, 256), 256)],
                preferred_element_type=F32,
            )
            high = dst_hi[k]
            both = []
            for part in range(2):
                mine = found[:, part * 128 : part * 128 + 128]
                h = rows_of(high[part : part + 1], 8)
                got = mine[0:8]
                for v in range(1, 8):
                    got = jnp.where(h == v, mine[v * 8 : v * 8 + 8], got)
                back_send[k, part] = got[0:4].astype(BF16)
                both.append(got)
            ends = jnp.where(sub < 2, pltpu.roll(both[0], 4, 0), pltpu.roll(both[1], 6, 0))
            back_send[k, 2] = ends[0:4].astype(BF16)
        start_all(back_copy)(i, first)

    each_group(answer)

    back_recv[0] = back_send[0]

    summed[...] = jnp.zeros_like(summed)

    def gather_up(i, spread2):
        here = pl.ds(pl.multiple_of(i * 2 * G, 2 * G), 2 * G)
        hi, w = src_hi[here, :], weight[here, :]
        for j in range(G):
            ends = back_recv[i * G + j, 2].astype(F32)
            for part in range(2):
                most = back_recv[i * G + j, part].astype(F32)
                last = [ends[2:4], ends[0:2]] if part else [ends]
                value = jnp.concatenate([most] + last, axis=0)
                value = value * rows_of(w[2 * j + part : 2 * j + part + 1], 8)
                top = value.astype(BF16).astype(F32)
                pair = jnp.concatenate([top, value - top], axis=0).astype(BF16)
                h = rows_of(hi[2 * j + part : 2 * j + part + 1], 16).astype(BF16)
                at = slice(j * 256 + part * 128, j * 256 + part * 128 + 128)
                for v in range(16):
                    spread2[v * 16 : v * 16 + 16, at] = jnp.where(h == v, pair, zero)
        added = lax.dot_general(
            spread2[...],
            hot_src[:, pl.ds(pl.multiple_of(i * width, width), width)],
            NT,
            preferred_element_type=F32,
        )
        summed[...] += added

    @pl.loop(0, groups // 2 - 1)
    def _(n):
        settle_group(back_recv, back_rs, 2 * n + 1, 0)
        settle_group(back_recv, back_rs, 2 * n + 2, 0)
        gather_up(2 * n + 1, spread2)
        gather_up(2 * n + 2, spread3)

    settle_group(back_recv, back_rs, groups - 1, 0)
    settle_group(back_recv, back_rs, 0, 1)
    gather_up(groups - 1, spread2)
    gather_up(0, spread3)

    for half in range(2):
        here = slice(half * 128, half * 128 + 128)
        for h in range(16):
            table32[half, h * 8 : h * 8 + 8, :] = (
                summed[h * 16 : h * 16 + 8, here] + summed[h * 16 + 8 : h * 16 + 16, here]
            )
        for s in range(6):
            atm_surf[s, :, here] = jnp.where(
                sea[:, here], table32[half, pl.ds(s, 16, stride=8), :], F32(0)
            )

    stores.append(pltpu.make_async_copy(atm_surf, surf_to, out_sem.at[2]))
    stores[2].start()
    for copy in stores:
        copy.wait()

    settle(dst_send, dst_ss, 1, devices - 1)
    settle(fwd_send, fwd_ss, 1, devices - 1)
    settle(back_send, back_ss, 1, devices - 1)


def hand_over(a, b, c, a_to, b_to, c_to, a_here, b_here, c_here, sem):
    here = (a_here.at[pl.ds(0, 8)], a_here.at[pl.ds(8, 8)], b_here, c_here)
    into = (a.at[pl.ds(0, 8)], a.at[pl.ds(8, 8)], b, c)
    out = (a_to.at[pl.ds(0, 8)], a_to.at[pl.ds(8, 8)], b_to, c_to)
    loads = [pltpu.make_async_copy(into[n], here[n], sem.at[n]) for n in range(4)]
    stores = [pltpu.make_async_copy(here[n], out[n], sem.at[4 + n]) for n in range(4)]
    for copy in loads:
        copy.start()
    for n in range(4):
        loads[n].wait()
        stores[n].start()
    for copy in stores:
        copy.wait()


def on_device(grps, tiles, *args):
    (
        atmos,
        diffusivity,
        sea_atm,
        flux_weight,
        block_owner,
        entry_count,
        source_col,
        dest_col,
        margin,
        ocean,
        sea_ocean,
        couple,
        surface_weight,
    ) = args
    devices = grps * tiles
    slots = 2 * devices
    vmem = pl.BlockSpec(memory_space=pltpu.VMEM)
    smem = pl.BlockSpec(memory_space=pltpu.SMEM)
    far = pl.BlockSpec(memory_space=pl.ANY)
    chans, rows, cols = atmos.shape
    dma = pltpu.SemaphoreType.DMA
    shapes = (
        jax.ShapeDtypeStruct(atmos.shape, F32),
        jax.ShapeDtypeStruct(ocean.shape, F32),
        jax.ShapeDtypeStruct((6, rows, cols), F32),
    )
    results = pl.pallas_call(
        functools.partial(kernel, grps, tiles),
        out_shape=shapes,
        in_specs=[far, far, far, smem, vmem, vmem, far, far, far, far, vmem, vmem, vmem],
        out_specs=(far, far, far),
        scratch_shapes=[
            pltpu.VMEM((chans, rows, cols), F32),
            pltpu.VMEM((rows, cols), F32),
            pltpu.VMEM((rows, cols), I32),
            pltpu.VMEM(source_col.shape, I32),
            pltpu.VMEM(source_col.shape, I32),
            pltpu.VMEM(source_col.shape, F32),
            pltpu.VMEM(ocean.shape, F32),
            pltpu.VMEM((chans, rows, cols), F32),
            pltpu.VMEM(ocean.shape, F32),
            pltpu.VMEM((6, rows, cols), F32),
            pltpu.VMEM((chans, rows, cols), F32),
            pltpu.VMEM((2, 2 * chans + 1, cols), F32),
            pltpu.VMEM((2, 2 * chans + 1, cols), F32),
            pltpu.VMEM((2, rows, 128), F32),
            pltpu.VMEM((2, rows, 128), F32),
            pltpu.VMEM((4, 8, 128), F32),
            pltpu.VMEM((slots, 128), F32),
            pltpu.VMEM((slots, 128), F32),
            pltpu.VMEM((slots, 128), F32),
            pltpu.VMEM((devices, 2, 128), F32),
            pltpu.VMEM((devices, 2, 128), F32),
            pltpu.VMEM((devices, 2, 128), F32),
            pltpu.VMEM((slots, 128), F32),
            pltpu.VMEM((256, slots * 128), BF16),
            pltpu.VMEM((128, slots * 128), BF16),
            pltpu.VMEM((2, 192, 128), F32),
            pltpu.VMEM((192, 256), BF16),
            pltpu.VMEM((devices, 3, 8, 128), BF16),
            pltpu.VMEM((devices, 3, 8, 128), BF16),
            pltpu.VMEM((128, G * 256), BF16),
            pltpu.VMEM((64, 128), F32),
            pltpu.VMEM((devices, 3, 4, 128), BF16),
            pltpu.VMEM((devices, 3, 4, 128), BF16),
            pltpu.VMEM((256, G * 256), BF16),
            pltpu.VMEM((256, G * 256), BF16),
            pltpu.VMEM((128, 128), F32),
            pltpu.VMEM((256, 256), F32),
            dma((8,)),
            dma((8,)),
            dma(()),
            dma(()),
            dma(()),
            dma((devices // G,)),
            dma(()),
            dma((devices // G,)),
            dma((11,)),
            dma((3,)),
        ],
        compiler_params=pltpu.CompilerParams(
            collective_id=0, has_side_effects=True, vmem_limit_bytes=56 * 1024 * 1024
        ),
    )(
        atmos,
        diffusivity,
        sea_atm,
        flux_weight,
        block_owner.reshape(1, -1),
        entry_count.reshape(1, -1),
        source_col,
        dest_col,
        margin,
        ocean,
        sea_ocean.reshape(1, -1),
        couple,
        surface_weight,
    )
    return pl.pallas_call(
        hand_over,
        out_shape=shapes,
        in_specs=[far] * 3,
        out_specs=(far, far, far),
        scratch_shapes=[pltpu.VMEM(x.shape, F32) for x in shapes] + [dma((8,))],
    )(*results)


def solution(mesh):
    placed = (
        P(None, "grp", "tile"),
        P("grp", "tile"),
        P("grp", "tile"),
        P(),
        P(("grp", "tile"), None),
        P(("grp", "tile")),
        P(("grp", "tile"), None),
        P(("grp", "tile"), None),
        P(("grp", "tile"), None),
        P(None, ("grp", "tile")),
        P(("grp", "tile")),
        P(),
        P(),
    )
    return jax.shard_map(
        functools.partial(on_device, mesh.shape["grp"], mesh.shape["tile"]),
        mesh=mesh,
        in_specs=placed,
        out_specs=(P(None, "grp", "tile"), P(None, ("grp", "tile")), P(None, "grp", "tile")),
        check_vma=False,
    )
```

```python
import functools

import jax
import jax.numpy as jnp
from jax import lax
from jax.experimental import pallas as pl
from jax.experimental.pallas import tpu as pltpu
from jax.sharding import PartitionSpec as P

MESH = pl.DeviceIdType.MESH
F32, BF16, I32 = jnp.float32, jnp.bfloat16, jnp.int32
NT = (((1,), (1,)), ((), ()))
G = 8


def iota(shape, dim):
    return lax.broadcasted_iota(I32, shape, dim)


def rows_of(row, count):
    return jnp.broadcast_to(row, (count, row.shape[1]))


def remote(src, dst, send_sem, recv_sem, device):
    return pltpu.make_async_remote_copy(
        src_ref=src,
        dst_ref=dst,
        send_sem=send_sem,
        recv_sem=recv_sem,
        device_id=device,
        device_id_type=MESH,
    )


def kernel(
    grps,
    tiles,
    atmos_in,
    kappa_in,
    sea_atm_in,
    flux_w,
    owner,
    count,
    source_in,
    dest_in,
    margin_in,
    ocean_in,
    sea_oc,
    couple,
    surf_w,
    atmos_to,
    ocean_to,
    surf_to,
    atmos,
    kappa,
    sea_atm,
    source,
    dest,
    margin,
    ocean,
    atmos_out,
    ocean_out,
    atm_surf,
    mid,
    row_send,
    row_recv,
    col_send,
    col_recv,
    corner_recv,
    src_hi,
    src_lo,
    dst_all,
    dst_send,
    dst_recv,
    dst_hi,
    weight,
    hot_src,
    hot_dst,
    table32,
    table,
    fwd_send,
    fwd_recv,
    spread,
    spread1,
    surf32,
    back_send,
    back_recv,
    spread2,
    spread3,
    total,
    summed,
    halo_ss,
    halo_rs,
    dst_ss,
    dst_rs,
    fwd_ss,
    fwd_rs,
    back_ss,
    back_rs,
    in_sem,
    out_sem,
):
    devices = grps * tiles
    groups = devices // G
    width = G * 256
    g, t = lax.axis_index("grp"), lax.axis_index("tile")
    me = g * tiles + t

    z, y, core = t // 8, lax.rem(t // 2, 4), lax.rem(t, 2)

    def peer(i, j, back=False):
        s, c = j // 2, j % 2
        dz, dy = i // 4 + s, lax.rem(i, 4) + s
        if back:
            s, dz, dy = 4 - s, 8 - dz, 8 - dy
        row = lax.rem(z + dz, 4) * 8 + lax.rem(y + dy, 4) * 2 + lax.rem(core + c, 2)
        return (lax.rem(g + s, 4), row)

    def dest_copy(i, j):
        k = i * G + j
        return remote(dst_send.at[k], dst_recv.at[k], dst_ss, dst_rs, peer(i, j))

    def fwd_copy(i, j):
        k = i * G + j
        return remote(fwd_send.at[k], fwd_recv.at[k], fwd_ss, fwd_rs.at[i], peer(i, j))

    def back_copy(i, j):
        k = i * G + j
        return remote(back_send.at[k], back_recv.at[k], back_ss, back_rs.at[i], peer(i, j, True))

    def each_group(act):
        @pl.loop(1, groups)
        def _(i):
            act(i, 0)

        act(0, 1)

    def start_all(make):
        def act(i, first):
            for j in range(first, G):
                make(i, j).start()

        return act

    def settle(buffer, sem, start, size):
        part = buffer.at[pl.ds(start, size)]
        pltpu.make_async_copy(part, part, sem).wait()

    def settle_group(buffer, sems, i, first):
        settle(buffer, sems.at[i], i * G + first, G - first)

    loads = {}
    for n, (name, a, b) in enumerate(
        (
            ("atmos", atmos_in, atmos),
            ("kappa", kappa_in, kappa),
            ("source", source_in, source),
            ("dest", dest_in, dest),
            ("margin", margin_in, margin),
            ("sea", sea_atm_in, sea_atm),
            ("ocean", ocean_in, ocean),
        )
    ):
        loads[name] = pltpu.make_async_copy(a, b, in_sem.at[n])
        loads[name].start()

    barrier = pltpu.get_barrier_semaphore()

    def greet(i, first):
        for j in range(first, G):
            pl.semaphore_signal(barrier, inc=1, device_id=peer(i, j), device_id_type=MESH)

    each_group(greet)

    ids16 = (iota((16, 16, 128), 0) * 16 + iota((16, 16, 128), 1)).astype(F32).astype(BF16)
    ids8 = (iota((8, 16, 128), 0) * 16 + iota((8, 16, 128), 1)).astype(F32).astype(BF16)
    one, zero = jnp.ones((16, 128), BF16), jnp.zeros((16, 128), BF16)

    def place_blocks():
        blocks = owner.shape[1]
        own_row = owner[...]
        own_here = jnp.broadcast_to(own_row, (blocks, blocks)).astype(F32)
        own_col = jnp.transpose(own_here)
        cnt_col = jnp.transpose(jnp.broadcast_to(count[...], (blocks, blocks)).astype(F32))
        before = iota((blocks, blocks), 0) < iota((blocks, blocks), 1)
        same = jnp.where((own_here == own_col) & before, F32(1), F32(0))
        rank = jnp.sum(same, axis=0, keepdims=True).astype(I32)
        dx = ((own_row >> 5) - g) & 3
        dz = (((own_row >> 3) & 3) - z - dx) & 3
        dy = (((own_row >> 1) & 3) - y - dx) & 3
        dc = ((own_row & 1) - core) & 1
        slot = (((dz * 4 + dy) * 4 + dx) * 2 + dc) * 2 + rank
        place = jnp.where(
            iota((2 * devices, blocks), 0) == jnp.broadcast_to(slot, (2 * devices, blocks)), F32(1), F32(0)
        ).astype(BF16)

        def placed(values):
            return jnp.dot(place, values.astype(BF16), preferred_element_type=F32)

        src = source[...]
        src_hi[...] = placed((src >> 8).astype(F32))
        src_lo[...] = placed((src & 255).astype(F32))
        dst = dest[...]
        dst_all[...] = placed((dst >> 7).astype(F32)) * 128.0 + placed((dst & 127).astype(F32))

        @pl.loop(0, devices // 4)
        def _(i):
            four = dst_all[pl.ds(pl.multiple_of(i * 8, 8), 8), :]
            for j in range(4):
                dst_send[i * 4 + j] = four[2 * j : 2 * j + 2]

        dst_recv[0] = dst_send[0]
        lanes = iota((blocks, 128), 1).astype(F32)
        live = jnp.where(lanes < cnt_col[:, :1], margin[...], F32(0))
        first = live.astype(BF16).astype(F32)
        rest = live - first
        second = rest.astype(BF16).astype(F32)
        third = rest - second
        weight[...] = placed(first) + placed(second) + placed(third)

    rows, cols = atmos.shape[1], atmos.shape[2]
    chans = atmos.shape[0]
    row_id, col_id = iota((rows, cols), 0), iota((rows, cols), 1)
    lane = iota((rows, 128), 1)
    up_g, down_g = lax.rem(g + grps - 1, grps), lax.rem(g + 1, grps)
    left_t, right_t = lax.rem(t + tiles - 1, tiles), lax.rem(t + 1, tiles)
    edge_n, edge_s, edge_w, edge_e = g == 0, g == grps - 1, t == 0, t == tiles - 1
    loads["atmos"].wait()
    loads["kappa"].wait()
    diffusion = kappa[...]
    west = jnp.where(lane == 2 * chans, diffusion[:, 0:1], F32(0))
    east = jnp.where(lane == 2 * chans, diffusion[:, cols - 1 : cols], F32(0))
    for ch in range(chans):
        x = atmos[ch]
        far_ch = chans + ch
        row_send[0, ch : ch + 1, :] = x[0:1]
        row_send[0, far_ch : far_ch + 1, :] = x[1:2]
        row_send[1, ch : ch + 1, :] = x[rows - 1 : rows]
        row_send[1, far_ch : far_ch + 1, :] = x[rows - 2 : rows - 1]
        west = jnp.where(lane == ch, x[:, 0:1], west)
        west = jnp.where(lane == far_ch, x[:, 1:2], west)
        east = jnp.where(lane == ch, x[:, cols - 1 : cols], east)
        east = jnp.where(lane == far_ch, x[:, cols - 2 : cols - 1], east)
    row_send[0, 2 * chans : 2 * chans + 1, :] = diffusion[0:1]
    row_send[1, 2 * chans : 2 * chans + 1, :] = diffusion[rows - 1 : rows]
    col_send[0] = west
    col_send[1] = east
    top, bottom = pl.ds(0, 8), pl.ds(rows - 8, 8)
    plan = (
        (row_send.at[0], row_recv.at[1], (up_g, t)),
        (row_send.at[1], row_recv.at[0], (down_g, t)),
        (col_send.at[0], col_recv.at[1], (g, left_t)),
        (col_send.at[1], col_recv.at[0], (g, right_t)),
        (col_send.at[0, top], corner_recv.at[3], (up_g, left_t)),
        (col_send.at[1, top], corner_recv.at[2], (up_g, right_t)),
        (col_send.at[0, bottom], corner_recv.at[1], (down_g, left_t)),
        (col_send.at[1, bottom], corner_recv.at[0], (down_g, right_t)),
    )
    copies = [
        remote(src, dst, halo_ss.at[n], halo_rs.at[n], device)
        for n, (src, dst, device) in enumerate(plan)
    ]
    pl.semaphore_wait(barrier, devices - 1)
    for copy in copies:
        copy.start()
    for name in ("source", "dest", "margin", "sea", "ocean"):
        loads[name].wait()
    place_blocks()
    each_group(start_all(dest_copy))
    for copy in copies:
        copy.wait()

    nw = jnp.where(edge_n | edge_w, F32(0), corner_recv[0, 7:8, :])
    ne = jnp.where(edge_n | edge_e, F32(0), corner_recv[1, 7:8, :])
    sw = jnp.where(edge_s | edge_w, F32(0), corner_recv[2, 0:1, :])
    se = jnp.where(edge_s | edge_e, F32(0), corner_recv[3, 0:1, :])

    def upright(row):
        spot = jnp.where(lane == iota((rows, 128), 0), jnp.broadcast_to(row, (rows, 128)), F32(0))
        return jnp.sum(spot, axis=1, keepdims=True)

    def line(here, below, above, at_left, at_right, rate):
        left = jnp.where(col_id == 0, upright(at_left), pltpu.roll(here, 1, 1))
        right = jnp.where(col_id == cols - 1, upright(at_right), pltpu.roll(here, cols - 1, 1))
        return here + rate * (below + above + right + left - 4.0 * here)

    row_lane = iota((rows, 128), 0)

    def column(here, right, left, at_top, at_bottom, rate):
        above = jnp.where(row_lane == 0, at_top, pltpu.roll(here, 1, 0))
        below = jnp.where(row_lane == rows - 1, at_bottom, pltpu.roll(here, rows - 1, 0))
        return here + rate * (below + above + right + left - 4.0 * here)

    north = jnp.where(edge_n, F32(0), row_recv[0, 0:chans, :])
    north2 = jnp.where(edge_n, F32(0), row_recv[0, chans : 2 * chans, :])
    south = jnp.where(edge_s, F32(0), row_recv[1, 0:chans, :])
    south2 = jnp.where(edge_s, F32(0), row_recv[1, chans : 2 * chans, :])
    west = jnp.where(edge_w, F32(0), col_recv[0])
    east = jnp.where(edge_e, F32(0), col_recv[1])
    rim = [
        (north, south, west, east),
        (
            jnp.where(
                edge_n,
                F32(0),
                line(
                    north,
                    row_send[0, 0:chans, :],
                    north2,
                    nw,
                    ne,
                    row_recv[0, 2 * chans : 2 * chans + 1, :],
                ),
            ),
            jnp.where(
                edge_s,
                F32(0),
                line(
                    south,
                    south2,
                    row_send[1, 0:chans, :],
                    sw,
                    se,
                    row_recv[1, 2 * chans : 2 * chans + 1, :],
                ),
            ),
            jnp.where(
                edge_w,
                F32(0),
                column(
                    west,
                    col_send[0],
                    pltpu.roll(west, 128 - chans, 1),
                    nw,
                    sw,
                    col_recv[0, :, 2 * chans : 2 * chans + 1],
                ),
            ),
            jnp.where(
                edge_e,
                F32(0),
                column(
                    east,
                    pltpu.roll(east, 128 - chans, 1),
                    col_send[1],
                    ne,
                    se,
                    col_recv[1, :, 2 * chans : 2 * chans + 1],
                ),
            ),
        ),
    ]
    for step in range(2):
        state, after = (atmos, mid) if step == 0 else (mid, atmos_out)
        north, south, west, east = rim[step]
        for ch in range(chans):
            x = state[ch]
            up = jnp.where(row_id == 0, north[ch : ch + 1], pltpu.roll(x, 1, 0))
            down = jnp.where(row_id == rows - 1, south[ch : ch + 1], pltpu.roll(x, rows - 1, 0))
            left = jnp.where(col_id == 0, west[:, ch : ch + 1], pltpu.roll(x, 1, 1))
            right = jnp.where(col_id == cols - 1, east[:, ch : ch + 1], pltpu.roll(x, cols - 1, 1))
            after[ch] = x + diffusion * (down + up + right + left - 4.0 * x)

    stores = [pltpu.make_async_copy(atmos_out, atmos_to, out_sem.at[0])]
    stores[0].start()

    sea = sea_atm[...] > 0
    for f in range(12):
        mixed = flux_w[f, 0] * atmos_out[0]
        for ch in range(1, chans):
            mixed = mixed + flux_w[f, ch] * atmos_out[ch]
        flux = jnp.where(sea, jnp.tanh(mixed), F32(0))
        for half in range(2):
            part = flux[:, half * 128 : half * 128 + 128]
            if f < 8:
                table32[half, pl.ds(f, 16, stride=8), :] = part
            else:
                table32[half, pl.ds(128 + f - 8, 16, stride=4), :] = part
    for half in range(2):
        full = table32[half]
        table[:, half * 128 : half * 128 + 128] = full.astype(BF16)

    sub = iota((8, 128), 0)
    odd = jnp.where(sub >= 4, F32(1), F32(0))

    def give(i, first):
        here = pl.ds(pl.multiple_of(i * 2 * G, 2 * G), 2 * G)
        low = src_lo[here, :]
        hi, w = src_hi[here, :], weight[here, :]
        for j in range(G):
            hots = []
            for part in range(2):
                lo = rows_of(low[2 * j + part : 2 * j + part + 1], 16).astype(BF16)
                hots.append(jnp.where(ids16 == lo[None], one[None], zero[None]).reshape(256, 128))
            hot = jnp.concatenate(hots, axis=1)
            hot_src[:, pl.ds(pl.multiple_of(i * width + j * 256, 256), 256)] = hot
            found = jnp.dot(table[...], hot, preferred_element_type=F32)
            ends = []
            for part in range(2):
                mine = found[:, part * 128 : part * 128 + 128]
                h = rows_of(hi[2 * j + part : 2 * j + part + 1], 8)
                wide = mine[0:8]
                for v in range(1, 16):
                    wide = jnp.where(h == v, mine[v * 8 : v * 8 + 8], wide)
                h = h - odd
                thin = jnp.zeros((8, 128), F32)
                for v in range(8):
                    thin = jnp.where(h == 2 * v, mine[128 + v * 8 : 136 + v * 8], thin)
                scale = rows_of(w[2 * j + part : 2 * j + part + 1], 8)
                fwd_send[i * G + j, part] = (wide * scale).astype(BF16)
                ends.append((thin + pltpu.roll(thin, 4, 0)) * scale)
            fwd_send[i * G + j, 2] = jnp.where(sub < 4, ends[0], ends[1]).astype(BF16)
        start_all(fwd_copy)(i, first)

    each_group(give)

    fwd_recv[0] = fwd_send[0]

    settle(dst_recv, dst_rs, 1, devices - 1)

    @pl.loop(0, groups)
    def _(i):
        for j in range(G):
            where = dst_recv[i * G + j]
            high = jnp.floor(where * (1 / 128))
            dst_hi[i * G + j] = high
            low = where - high * 128.0
            for part in range(2):
                lo = rows_of(low[part : part + 1], 16).astype(BF16)
                hot = jnp.where(ids8 == lo[None], one[None], zero[None])
                hot_dst[:, pl.ds(pl.multiple_of(i * width + j * 256 + part * 128, 128), 128)] = hot.reshape(
                    128, 128
                )

    total[...] = jnp.zeros_like(total)

    def collect(i, spread):
        for j in range(G):
            high = dst_hi[i * G + j]
            ends = fwd_recv[i * G + j, 2].astype(F32)
            for part in range(2):
                tile = jnp.concatenate(
                    [fwd_recv[i * G + j, part].astype(F32), pltpu.roll(ends, 4, 0) if part else ends],
                    axis=0,
                ).astype(BF16)
                hi = rows_of(high[part : part + 1], 16).astype(BF16)
                at = slice(j * 256 + part * 128, j * 256 + part * 128 + 128)
                for v in range(8):
                    spread[v * 16 : v * 16 + 16, at] = jnp.where(hi == v, tile, zero)
        total[...] += lax.dot_general(
            spread[...],
            hot_dst[:, pl.ds(pl.multiple_of(i * width, width), width)],
            NT,
            preferred_element_type=F32,
        )

    @pl.loop(0, groups // 2 - 1)
    def _(n):
        settle_group(fwd_recv, fwd_rs, 2 * n + 1, 0)
        settle_group(fwd_recv, fwd_rs, 2 * n + 2, 0)
        collect(2 * n + 1, spread)
        collect(2 * n + 2, spread1)

    settle_group(fwd_recv, fwd_rs, groups - 1, 0)
    settle_group(fwd_recv, fwd_rs, 0, 1)
    collect(groups - 1, spread)
    collect(0, spread1)

    surf32[...] = jnp.zeros_like(surf32)
    for h in range(8):
        here = slice(h * 128, h * 128 + 128)
        flux = total[h * 16 : h * 16 + 16, :]
        added = couple[:, 0:1] * flux[0:1]
        for f in range(1, 12):
            added = added + couple[:, f : f + 1] * flux[f : f + 1]
        new = ocean[:, here] + jnp.where(sea_oc[:, here] > 0, added, F32(0))
        ocean_out[:, here] = new
        field = surf_w[:, 0:1] * new[0:1]
        for o in range(1, 8):
            field = field + surf_w[:, o : o + 1] * new[o : o + 1]
        surf32[h * 8 : h * 8 + 6, :] = jnp.tanh(field)
    surface = surf32[...].astype(BF16)
    stores.append(pltpu.make_async_copy(ocean_out, ocean_to, out_sem.at[1]))
    stores[1].start()

    def answer(i, first):
        for j in range(G):
            k = i * G + j
            found = jnp.dot(
                surface,
                hot_dst[:, pl.ds(pl.multiple_of(i * width + j * 256, 256), 256)],
                preferred_element_type=F32,
            )
            high = dst_hi[k]
            both = []
            for part in range(2):
                mine = found[:, part * 128 : part * 128 + 128]
                h = rows_of(high[part : part + 1], 8)
                got = mine[0:8]
                for v in range(1, 8):
                    got = jnp.where(h == v, mine[v * 8 : v * 8 + 8], got)
                back_send[k, part] = got[0:4].astype(BF16)
                both.append(got)
            ends = jnp.where(sub < 2, pltpu.roll(both[0], 4, 0), pltpu.roll(both[1], 6, 0))
            back_send[k, 2] = ends[0:4].astype(BF16)
        start_all(back_copy)(i, first)

    each_group(answer)

    back_recv[0] = back_send[0]

    summed[...] = jnp.zeros_like(summed)

    def gather_up(i, spread2):
        here = pl.ds(pl.multiple_of(i * 2 * G, 2 * G), 2 * G)
        hi, w = src_hi[here, :], weight[here, :]
        for j in range(G):
            ends = back_recv[i * G + j, 2].astype(F32)
            for part in range(2):
                most = back_recv[i * G + j, part].astype(F32)
                last = [ends[2:4], ends[0:2]] if part else [ends]
                value = jnp.concatenate([most] + last, axis=0)
                value = value * rows_of(w[2 * j + part : 2 * j + part + 1], 8)
                top = value.astype(BF16).astype(F32)
                pair = jnp.concatenate([top, value - top], axis=0).astype(BF16)
                h = rows_of(hi[2 * j + part : 2 * j + part + 1], 16).astype(BF16)
                at = slice(j * 256 + part * 128, j * 256 + part * 128 + 128)
                for v in range(16):
                    spread2[v * 16 : v * 16 + 16, at] = jnp.where(h == v, pair, zero)
        added = lax.dot_general(
            spread2[...],
            hot_src[:, pl.ds(pl.multiple_of(i * width, width), width)],
            NT,
            preferred_element_type=F32,
        )
        summed[...] += added

    @pl.loop(0, groups // 2 - 1)
    def _(n):
        settle_group(back_recv, back_rs, 2 * n + 1, 0)
        settle_group(back_recv, back_rs, 2 * n + 2, 0)
        gather_up(2 * n + 1, spread2)
        gather_up(2 * n + 2, spread3)

    settle_group(back_recv, back_rs, groups - 1, 0)
    settle_group(back_recv, back_rs, 0, 1)
    gather_up(groups - 1, spread2)
    gather_up(0, spread3)

    for half in range(2):
        here = slice(half * 128, half * 128 + 128)
        for h in range(16):
            table32[half, h * 8 : h * 8 + 8, :] = (
                summed[h * 16 : h * 16 + 8, here] + summed[h * 16 + 8 : h * 16 + 16, here]
            )
        for s in range(6):
            atm_surf[s, :, here] = jnp.where(
                sea[:, here], table32[half, pl.ds(s, 16, stride=8), :], F32(0)
            )

    stores.append(pltpu.make_async_copy(atm_surf, surf_to, out_sem.at[2]))
    stores[2].start()
    for copy in stores:
        copy.wait()

    settle(dst_send, dst_ss, 1, devices - 1)
    settle(fwd_send, fwd_ss, 1, devices - 1)
    settle(back_send, back_ss, 1, devices - 1)


def hand_over(a, b, c, a_to, b_to, c_to, a_here, b_here, c_here, sem):
    here = (a_here.at[pl.ds(0, 8)], a_here.at[pl.ds(8, 8)], b_here, c_here)
    into = (a.at[pl.ds(0, 8)], a.at[pl.ds(8, 8)], b, c)
    out = (a_to.at[pl.ds(0, 8)], a_to.at[pl.ds(8, 8)], b_to, c_to)
    loads = [pltpu.make_async_copy(into[n], here[n], sem.at[n]) for n in range(4)]
    stores = [pltpu.make_async_copy(here[n], out[n], sem.at[4 + n]) for n in range(4)]
    for copy in loads:
        copy.start()
    for n in range(4):
        loads[n].wait()
        stores[n].start()
    for copy in stores:
        copy.wait()


def on_device(grps, tiles, *args):
    (
        atmos,
        diffusivity,
        sea_atm,
        flux_weight,
        block_owner,
        entry_count,
        source_col,
        dest_col,
        margin,
        ocean,
        sea_ocean,
        couple,
        surface_weight,
    ) = args
    devices = grps * tiles
    slots = 2 * devices
    vmem = pl.BlockSpec(memory_space=pltpu.VMEM)
    smem = pl.BlockSpec(memory_space=pltpu.SMEM)
    far = pl.BlockSpec(memory_space=pl.ANY)
    chans, rows, cols = atmos.shape
    dma = pltpu.SemaphoreType.DMA
    shapes = (
        jax.ShapeDtypeStruct(atmos.shape, F32),
        jax.ShapeDtypeStruct(ocean.shape, F32),
        jax.ShapeDtypeStruct((6, rows, cols), F32),
    )
    results = pl.pallas_call(
        functools.partial(kernel, grps, tiles),
        out_shape=shapes,
        in_specs=[far, far, far, smem, vmem, vmem, far, far, far, far, vmem, vmem, vmem],
        out_specs=(far, far, far),
        scratch_shapes=[
            pltpu.VMEM((chans, rows, cols), F32),
            pltpu.VMEM((rows, cols), F32),
            pltpu.VMEM((rows, cols), I32),
            pltpu.VMEM(source_col.shape, I32),
            pltpu.VMEM(source_col.shape, I32),
            pltpu.VMEM(source_col.shape, F32),
            pltpu.VMEM(ocean.shape, F32),
            pltpu.VMEM((chans, rows, cols), F32),
            pltpu.VMEM(ocean.shape, F32),
            pltpu.VMEM((6, rows, cols), F32),
            pltpu.VMEM((chans, rows, cols), F32),
            pltpu.VMEM((2, 2 * chans + 1, cols), F32),
            pltpu.VMEM((2, 2 * chans + 1, cols), F32),
            pltpu.VMEM((2, rows, 128), F32),
            pltpu.VMEM((2, rows, 128), F32),
            pltpu.VMEM((4, 8, 128), F32),
            pltpu.VMEM((slots, 128), F32),
            pltpu.VMEM((slots, 128), F32),
            pltpu.VMEM((slots, 128), F32),
            pltpu.VMEM((devices, 2, 128), F32),
            pltpu.VMEM((devices, 2, 128), F32),
            pltpu.VMEM((devices, 2, 128), F32),
            pltpu.VMEM((slots, 128), F32),
            pltpu.VMEM((256, slots * 128), BF16),
            pltpu.VMEM((128, slots * 128), BF16),
            pltpu.VMEM((2, 192, 128), F32),
            pltpu.VMEM((192, 256), BF16),
            pltpu.VMEM((devices, 3, 8, 128), BF16),
            pltpu.VMEM((devices, 3, 8, 128), BF16),
            pltpu.VMEM((128, G * 256), BF16),
            pltpu.VMEM((128, G * 256), BF16),
            pltpu.VMEM((64, 128), F32),
            pltpu.VMEM((devices, 3, 4, 128), BF16),
            pltpu.VMEM((devices, 3, 4, 128), BF16),
            pltpu.VMEM((256, G * 256), BF16),
            pltpu.VMEM((256, G * 256), BF16),
            pltpu.VMEM((128, 128), F32),
            pltpu.VMEM((256, 256), F32),
            dma((8,)),
            dma((8,)),
            dma(()),
            dma(()),
            dma(()),
            dma((devices // G,)),
            dma(()),
            dma((devices // G,)),
            dma((11,)),
            dma((3,)),
        ],
        compiler_params=pltpu.CompilerParams(
            collective_id=0, has_side_effects=True, vmem_limit_bytes=56 * 1024 * 1024
        ),
    )(
        atmos,
        diffusivity,
        sea_atm,
        flux_weight,
        block_owner.reshape(1, -1),
        entry_count.reshape(1, -1),
        source_col,
        dest_col,
        margin,
        ocean,
        sea_ocean.reshape(1, -1),
        couple,
        surface_weight,
    )
    return pl.pallas_call(
        hand_over,
        out_shape=shapes,
        in_specs=[far] * 3,
        out_specs=(far, far, far),
        scratch_shapes=[pltpu.VMEM(x.shape, F32) for x in shapes] + [dma((8,))],
    )(*results)


def solution(mesh):
    placed = (
        P(None, "grp", "tile"),
        P("grp", "tile"),
        P("grp", "tile"),
        P(),
        P(("grp", "tile"), None),
        P(("grp", "tile")),
        P(("grp", "tile"), None),
        P(("grp", "tile"), None),
        P(("grp", "tile"), None),
        P(None, ("grp", "tile")),
        P(("grp", "tile")),
        P(),
        P(),
    )
    return jax.shard_map(
        functools.partial(on_device, mesh.shape["grp"], mesh.shape["tile"]),
        mesh=mesh,
        in_specs=placed,
        out_specs=(P(None, "grp", "tile"), P(None, ("grp", "tile")), P(None, "grp", "tile")),
        check_vma=False,
    )
```
